256 devices in a mesh: layer: 32 (over z, x), batch: 8 (over y, core).
Axes of the slice: x: 4, y: 4, z: 8, core: 2. Of those that a mesh axis runs over, the one named last changes fastest.
Arguments:
- inputs: float32 [8, 8, 8, 8, 128], P('batch'), parts along dimension 0, may hold values from -6 to 6
- guess_states: float32 [128, 8, 8, 8, 8, 128], P('layer', 'batch'), parts along dimension 1, may hold values from -6 to 6
- kernels: bfloat16 [128, 3, 3, 3, 128, 128], P('layer'), may hold values from -0.109375 to 0.109375
- biases: float32 [128, 128], P('layer'), may hold values from -4 to 4
Outputs:
- states: float32 [128, 8, 8, 8, 8, 128], P('layer', 'batch'), parts along dimension 1
- coarse_residual: float32 [32, 8, 8, 8, 8, 128], P('layer', 'batch'), parts along dimension 1
The draws below stay inside these ranges and needn't reach their ends.
There are 8 independent parts, one for each index of `batch`. The reference program is written for one: setup_inputs(seed, part) draws one part's arguments, and reference() takes and returns one part's arrays. A program takes and returns all parts, laid end to end along the dimension named above; an argument that names none is the same for every part. Nothing has to cross between parts.
All inputs are finite; a program needn't handle non-finite values.
Results may differ from the reference program's by a relative error of at most 0.0008.
Values may be sent and summed in bfloat16 or wider, within the bound.
No kernel may reach another device: no remote copies, remote signals or barrier semaphores. Data moves between devices by JAX's collectives and lax.ppermute only.
A program may use at most 128 MiB of HBM per device.

```python
import jax
import jax.numpy as jnp
from jax import lax

CHANNELS = 128
VX = 8
VY = 8
VZ = 8
CLIPS = 1
SECT = 4
COARSEN = 4
LAYERS = 128
N_LAYER = 32


def level_of(stream_key, shape, cuts, low, high):
    def one(dim, blocks):
        steps = jax.random.uniform(jax.random.fold_in(jax.random.fold_in(stream_key, 6), dim), (blocks,), jnp.float32, low / len(cuts), high / len(cuts))
        return jnp.repeat(jnp.exp(steps), shape[dim] // blocks).reshape((-1,) + (1,) * (len(shape) - dim - 1))

    level = one(*cuts[0])
    for cut in cuts[1:]:
        level = level * one(*cut)
    return level


def bell_draw(stream_key, extent, scale, bound, shards=(), held_as=jnp.bfloat16):
    drawn = jax.random.normal(stream_key, extent, jnp.float32) * scale
    if len(shards) > 0:
        drawn = level_of(stream_key, extent, shards, -0.22, 0.18) * drawn
    return jnp.clip(drawn, min=-bound, max=bound).astype(held_as)


def setup_inputs(seed: int = 0, part: int = 0) -> dict:
    key_list = jax.random.split(jax.random.key(seed), 5)
    part_keys = jax.random.split(jax.random.fold_in(key_list[4], part), 5)
    inputs = bell_draw(part_keys[0], (CLIPS, VX, VY, VZ, CHANNELS), 1.0, 6.0, (), jnp.float32)
    guess_states = bell_draw(part_keys[1], (LAYERS, CLIPS, VX, VY, VZ, CHANNELS), 1.0, 6.0, ((0, 32),), jnp.float32)
    kernels = bell_draw(key_list[2], (LAYERS, 3, 3, 3, CHANNELS, CHANNELS), (27 * CHANNELS) ** -0.5, 0.109375, ((0, 32),))
    biases = bell_draw(key_list[3], (LAYERS, CHANNELS), 1.0, 4.0, ((0, 32),), jnp.float32)
    return dict(inputs=inputs, guess_states=guess_states, kernels=kernels, biases=biases)


def advance(state, kernel, offset_row, step_size):
    squashed = lax.optimization_barrier(jnp.tanh(state).astype(jnp.bfloat16)).astype(jnp.float32)
    count, size_x, size_y, size_z, width = state.shape
    padded = jnp.pad(squashed, ((0, 0), (1, 1), (1, 1), (1, 1), (0, 0)))
    pieces = []
    for shift_a in range(3):
        for shift_b in range(3):
            for shift_d in range(3):
                pieces.append(padded[:, shift_a:shift_a + size_x, shift_b:shift_b + size_y, shift_d:shift_d + size_z, :])
    columns = jnp.concatenate(pieces, -1).reshape((-1, 27 * width))
    matrix = kernel.astype(jnp.float32).reshape((27 * width, kernel.shape[-1]))
    mixed = jnp.dot(columns, matrix, precision=lax.Precision.HIGHEST, preferred_element_type=jnp.float32)
    mixed = mixed.reshape((count, size_x, size_y, size_z, kernel.shape[-1]))
    return state + step_size * (mixed + offset_row)


def reference(inputs, guess_states, kernels, biases):
    sections = N_LAYER
    depth = SECT
    groups = sections // COARSEN
    fine_size = 2.0 / (SECT * N_LAYER)
    coarse_size = depth * fine_size
    top_size = COARSEN * coarse_size
    stepper = jax.vmap(advance, in_axes=(0, 0, 0, None))
    tail = guess_states.shape[1:]
    states = guess_states.reshape((sections, depth) + tail)
    kernel_grid = kernels.reshape((sections, depth) + kernels.shape[1:])
    bias_grid = biases.reshape((sections, depth, biases.shape[-1]))

    def heads_of(current):
        return jnp.concatenate([inputs[None], current[:-1, -1]], 0)

    def relax_fine(current):
        chain_rows = [heads_of(current)]
        for layer_row in range(1, depth):
            chain_rows.append(stepper(chain_rows[-1], kernel_grid[:, layer_row - 1], bias_grid[:, layer_row - 1], fine_size))
        return jnp.stack(chain_rows[1:] + [current[:, -1]], 1)

    def settle_fine(current):
        corner = stepper(current[:, -2], kernel_grid[:, -1], bias_grid[:, -1], fine_size)
        return current.at[:, -1].set(corner)

    states = relax_fine(settle_fine(relax_fine(states)))
    heads = heads_of(states)
    fine_defect = stepper(states[:, -2], kernel_grid[:, -1], bias_grid[:, -1], fine_size) - stepper(heads, kernel_grid[:, 0], bias_grid[:, 0], coarse_size)

    coarse_values = states[:, -1].reshape((groups, COARSEN) + tail)
    coarse_defect = fine_defect.reshape((groups, COARSEN) + tail)
    coarse_kernels = kernel_grid[:, 0].reshape((groups, COARSEN) + kernels.shape[1:])
    coarse_biases = bias_grid[:, 0].reshape((groups, COARSEN, biases.shape[-1]))

    def coarse_heads(current):
        return jnp.concatenate([inputs[None], current[:-1, -1]], 0)

    def relax_coarse(current):
        chain_rows = [coarse_heads(current)]
        for turn in range(COARSEN - 1):
            chain_rows.append(stepper(chain_rows[-1], coarse_kernels[:, turn], coarse_biases[:, turn], coarse_size) + coarse_defect[:, turn])
        return jnp.stack(chain_rows[1:] + [current[:, -1]], 1)

    def settle_coarse(current):
        corner = stepper(current[:, -2], coarse_kernels[:, -1], coarse_biases[:, -1], coarse_size) + coarse_defect[:, -1]
        return current.at[:, -1].set(corner)

    coarse_values = relax_coarse(settle_coarse(relax_coarse(coarse_values)))
    group_heads = coarse_heads(coarse_values)
    flat_values = coarse_values.reshape((sections,) + tail)
    flat_heads = jnp.concatenate([inputs[None], flat_values[:-1]], 0)
    corner_all = stepper(flat_heads, kernel_grid[:, 0], bias_grid[:, 0], coarse_size) + fine_defect
    coarse_residual = corner_all - flat_values
    corner_owner = corner_all.reshape((groups, COARSEN) + tail)[:, -1]
    level_defect = corner_owner - stepper(group_heads, coarse_kernels[:, -1], coarse_biases[:, -1], top_size)

    level_two = inputs
    solved = []
    for turn in range(groups):
        level_two = advance(level_two, coarse_kernels[turn, -1], coarse_biases[turn, -1], top_size) + level_defect[turn]
        solved.append(level_two)
    coarse_values = coarse_values.at[:, -1].set(jnp.stack(solved, 0))
    coarse_values = relax_coarse(coarse_values)

    states = states.at[:, -1].set(coarse_values.reshape((sections,) + tail))
    states = relax_fine(states)
    return states.reshape(guess_states.shape), coarse_residual
```

```python
import functools

import jax
import jax.numpy as jnp
from jax import lax
from jax.experimental import pallas as pl
from jax.experimental.pallas import tpu as pltpu
from jax.sharding import Mesh
from jax.sharding import PartitionSpec as P

X, Z = 4, 8
LAYER, BATCH = ("z", "x"), ("y", "core")
ROWS, CH = 512, 128
TAPS, DEEP = 9, 384
SHARE = TAPS * DEEP // 8
FINE = 2.0 / 128
COARSE = 4 * FINE
TOP = 4 * COARSE


def conv(v, weights):
    t = jnp.tanh(v).reshape(64, 8, CH)
    at = lax.broadcasted_iota(jnp.int32, (64, 8, CH), 1)
    before = jnp.where(at == 0, 0.0, pltpu.roll(t, 1, 1))
    after = jnp.where(at == 7, 0.0, pltpu.roll(t, 7, 1))
    lhs = jnp.concatenate(
        [s.reshape(ROWS, CH).astype(jnp.bfloat16) for s in (before, t, after)], 1
    )
    rhs = jnp.concatenate([weights[n * DEEP : (n + 1) * DEEP] for n in range(TAPS)], 1)
    out = jnp.dot(lhs, rhs, preferred_element_type=jnp.float32)
    edge_y = jnp.zeros((8, 1, 8, CH), jnp.float32)
    edge_x = jnp.zeros((1, 8, 8, CH), jnp.float32)
    total = None
    for dx in range(3):
        for dy in range(3):
            n = dx * 3 + dy
            part = out[:, n * CH : (n + 1) * CH].reshape(8, 8, 8, CH)
            if dy == 0:
                part = jnp.concatenate([edge_y, part[:, :7]], 1)
            if dy == 2:
                part = jnp.concatenate([part[:, 1:], edge_y], 1)
            if dx == 0:
                part = jnp.concatenate([edge_x, part[:7]], 0)
            if dx == 2:
                part = jnp.concatenate([part[1:], edge_x], 0)
            total = part if total is None else total + part
    return total.reshape(ROWS, CH)


def own_weights(ref, index):
    return ref[pl.ds(index, 1)].reshape(TAPS * DEEP, CH)


def group_weights(ref, pos, q):
    turn = lax.rem(q - pos[0] + X, X)
    return ref[:, pl.ds(turn, 1)].reshape(TAPS * DEEP, CH)


def add_term(buf, pos, q, terms):
    turn = lax.rem(q - pos[0] + X, X)
    for r, term in enumerate(terms):

        @pl.when(turn == r)
        def _():
            buf[...] += term[...]


def first_kernel(pos, guess, head, inputs, kernels, biases, out):
    out[...] = jnp.where((pos[0] == 0) & (pos[1] == 0), inputs[...], head[...])

    def body(i, carry):
        v = out[...]
        out[...] = v + FINE * (conv(v, own_weights(kernels, i)) + biases[pl.ds(i, 1)])
        return carry

    lax.fori_loop(0, 4, body, 0)


def second_kernel(pos, head, inputs, kernels, biases, message, term, buf):
    start = jnp.where((pos[0] == 0) & (pos[1] == 0), inputs[...], head[...])
    buf[...] = start
    term[...] = start

    def body(i, carry):
        v = buf[...]
        mixed = conv(v, own_weights(kernels, i))
        buf[...] = v + FINE * (mixed + biases[pl.ds(i, 1)])

        @pl.when(i == 0)
        def _():
            term[...] += COARSE * mixed

        return carry

    lax.fori_loop(0, 4, body, 0)
    term[...] = buf[...] - term[...]

    @pl.when(pos[0] == 0)
    def _():
        message[...] = buf[...]

    @pl.when(pos[0] != 0)
    def _():
        message[...] = term[...]


def third_kernel(pos, m0, m1, m2, m3, weights, out):
    messages = (m0, m1, m2, m3)
    out[...] = jnp.zeros((ROWS, CH), jnp.float32)
    add_term(out, pos, 0, messages)

    def body(q, carry):
        out[...] += COARSE * conv(out[...], group_weights(weights, pos, q))
        add_term(out, pos, q, messages)
        return carry

    lax.fori_loop(1, 4, body, 0)


def first_term(pos, buf, own, f1, f2, f3):
    for x, term in enumerate((own, f1, f2, f3)):

        @pl.when(pos[0] == x)
        def _():
            buf[...] += term[...]


def fourth_kernel(
    pos, hop, inputs, point, own, f1, f2, f3, m1, m2, m3, weights, residual, corner, defect
):
    start = jnp.where(pos[1] == 0, inputs[...], hop[...])
    corner[...] = start
    residual[...] = jnp.zeros((ROWS, CH), jnp.float32)

    def body(q, carry):
        corner[...] += COARSE * conv(corner[...], group_weights(weights, pos, q))

        @pl.when(q == 0)
        def _():
            first_term(pos, corner, own, f1, f2, f3)

        @pl.when(q > 0)
        def _():
            add_term(corner, pos, q, (own, m1, m2, m3))

        return carry

    lax.fori_loop(0, 4, body, 0)

    @pl.when(pos[0] == 3)
    def _():
        residual[...] = corner[...] - point[...]

    start = jnp.where(pos[1] == 0, inputs[...], hop[...])
    defect[...] = corner[...] - start - TOP * conv(start, group_weights(weights, pos, 3))


def chain_kernel(step, pos, arrived, before, value, defect, weights, out_before, out_value):
    @pl.when(pos[1] == step)
    def _():
        v = arrived[...]
        out_before[...] = v
        out_value[...] = v + TOP * conv(v, group_weights(weights, pos, 3)) + defect[...]

    @pl.when(pos[1] != step)
    def _():
        out_before[...] = before[...]
        out_value[...] = value[...]


def last_kernel(
    pos, start, value, own, f1, f2, f3, m1, m2, m3, weights, kernels, biases, states, buf
):
    buf[...] = start[...]

    def coarse(q, carry):
        buf[...] += COARSE * conv(buf[...], group_weights(weights, pos, q))

        @pl.when(q == 0)
        def _():
            first_term(pos, buf, own, f1, f2, f3)

        @pl.when(q > 0)
        def _():
            add_term(buf, pos, q, (own, m1, m2, m3))

        return carry

    lax.fori_loop(0, pos[0], coarse, 0)

    def fine(i, carry):
        v = buf[...]
        mixed = conv(v, own_weights(kernels, i))

        @pl.when((i == 0) & (pos[0] < 3))
        def _():
            states[3] = v + COARSE * mixed + own[...]

        new = v + FINE * (mixed + biases[pl.ds(i, 1)])
        states[pl.ds(i, 1)] = new.reshape(1, ROWS, CH)
        buf[...] = new
        return carry

    lax.fori_loop(0, 3, fine, 0)

    @pl.when(pos[0] == 3)
    def _():
        states[3] = value[...]


STATE = jax.ShapeDtypeStruct((ROWS, CH), jnp.float32)


def call(body, name, outs, convs, *args, scratch=()):
    vmem = pl.BlockSpec(memory_space=pltpu.VMEM)
    smem = pl.BlockSpec(memory_space=pltpu.SMEM)
    return pl.pallas_call(
        body,
        name=name,
        out_shape=outs,
        in_specs=[smem] + [vmem] * (len(args) - 1),
        out_specs=jax.tree.map(lambda _: vmem, outs),
        scratch_shapes=scratch,
        compiler_params=pltpu.CompilerParams(vmem_limit_bytes=24 << 20),
        cost_estimate=pl.CostEstimate(
            flops=convs * 2 * ROWS * CH * CH * 27,
            bytes_accessed=convs * 27 * CH * CH * 2,
            transcendentals=convs * ROWS * CH,
        ),
    )(*args)


def shards(inputs, guess_states, kernels, biases):
    x, z = lax.axis_index("x"), lax.axis_index("z")
    pos = jnp.stack([x, z]).astype(jnp.int32)
    share_index = lax.axis_index(BATCH)
    state = jax.ShapeDtypeStruct((ROWS, CH), jnp.float32)
    buffer = pltpu.VMEM((ROWS, CH), jnp.float32)
    inputs = inputs.reshape(ROWS, CH)
    guess = guess_states[-1].reshape(ROWS, CH)
    kernels = kernels.reshape(4, TAPS * DEEP, CH)

    along = [(i, i + 1) for i in range(X * Z - 1)]
    ring = [[(i, (i - r) % X) for i in range(X)] for r in range(X)]

    def next_layer(v):
        return lax.ppermute(v, LAYER, along)

    def from_ahead(v, r):
        return lax.ppermute(v, "x", ring[r])

    head = next_layer(guess)
    share = lax.dynamic_slice_in_dim(kernels[0], share_index * SHARE, SHARE, 0)
    shares = jnp.stack([share] + [from_ahead(share, r) for r in (1, 2, 3)])
    group = lax.all_gather(shares, BATCH)

    point = call(first_kernel, "first", state, 4, pos, guess, head, inputs, kernels, biases)
    head = next_layer(point)
    message, term = call(
        second_kernel, "second", (state, state), 4, pos, head, inputs, kernels, biases,
        scratch=[buffer],
    )
    m1, m2, m3 = (from_ahead(message, r) for r in (1, 2, 3))
    point = call(third_kernel, "third", state, 3, pos, message, m1, m2, m3, group)
    hop = lax.ppermute(point, "z", [(i, i + 1) for i in range(Z - 1)])
    f1, f2, f3 = (lax.ppermute(term, "x", [(0, i)]) for i in (1, 2, 3))
    residual, corner, defect = call(
        fourth_kernel, "fourth", (state,) * 3, 5,
        pos, hop, inputs, point, term, f1, f2, f3, m1, m2, m3, group,
    )
    before = jnp.where(z == 0, inputs, hop)
    value = corner
    for step in range(2, Z):
        arrived = lax.ppermute(value, "z", [(step - 1, step)])
        before, value = call(
            functools.partial(chain_kernel, step), "chain", (state, state), 1,
            pos, arrived, before, value, defect, group,
        )
    states = call(
        last_kernel, "last", jax.ShapeDtypeStruct((4, ROWS, CH), jnp.float32), 6,
        pos, before, value, term, f1, f2, f3, m1, m2, m3, group, kernels, biases,
        scratch=[buffer],
    )
    volume = (8, 8, 8, CH)
    return states.reshape((4, 1) + volume), residual.reshape((1, 1) + volume)


def solution(mesh):
    finer = Mesh(mesh.devices.reshape(Z, X, 4, 2), LAYER + BATCH)
    return jax.shard_map(
        shards,
        mesh=finer,
        in_specs=(P(BATCH), P(LAYER, BATCH), P(LAYER), P(LAYER)),
        out_specs=(P(LAYER, BATCH), P(LAYER, BATCH)),
        check_vma=False,
    )
```

```python
import functools

import jax
import jax.numpy as jnp
from jax import lax
from jax.experimental import pallas as pl
from jax.experimental.pallas import tpu as pltpu
from jax.sharding import Mesh
from jax.sharding import PartitionSpec as P

X, Z = 4, 8
LAYER, BATCH = ("z", "x"), ("y", "core")
ROWS, CH = 512, 128
TAPS, DEEP = 9, 384
HALF = TAPS * DEEP // 2
WHOLE = (2, HALF, CH)
FINE = 2.0 / 128
COARSE = 4 * FINE
TOP = 4 * COARSE


def conv(v, weights):
    t = jnp.tanh(v).reshape(64, 8, CH)
    at = lax.broadcasted_iota(jnp.int32, (64, 8, CH), 1)
    before = jnp.where(at == 0, 0.0, pltpu.roll(t, 1, 1))
    after = jnp.where(at == 7, 0.0, pltpu.roll(t, 7, 1))
    lhs = jnp.concatenate(
        [s.reshape(ROWS, CH).astype(jnp.bfloat16) for s in (before, t, after)], 1
    )
    rhs = jnp.concatenate([weights[n * DEEP : (n + 1) * DEEP] for n in range(TAPS)], 1)
    out = jnp.dot(lhs, rhs, preferred_element_type=jnp.float32)
    edge_y = jnp.zeros((8, 1, 8, CH), jnp.float32)
    edge_x = jnp.zeros((1, 8, 8, CH), jnp.float32)
    total = None
    for dx in range(3):
        for dy in range(3):
            n = dx * 3 + dy
            part = out[:, n * CH : (n + 1) * CH].reshape(8, 8, 8, CH)
            if dy == 0:
                part = jnp.concatenate([edge_y, part[:, :7]], 1)
            if dy == 2:
                part = jnp.concatenate([part[:, 1:], edge_y], 1)
            if dx == 0:
                part = jnp.concatenate([edge_x, part[:7]], 0)
            if dx == 2:
                part = jnp.concatenate([part[1:], edge_x], 0)
            total = part if total is None else total + part
    return total.reshape(ROWS, CH)


def flat(weights):
    return weights.reshape(TAPS * DEEP, CH)


def relative(q):
    return lax.rem(q - lax.axis_index("x") + X, X)


def start_own(kernels, layer, slot, sem):
    for half in range(2):
        pltpu.make_async_copy(kernels.at[layer, half], slot.at[half], sem.at[half]).start()


def start_lead(q, slot, sem, mine, other):
    core = lax.axis_index("core")
    pltpu.make_async_copy(mine.at[q], slot.at[core], sem.at[core]).start()
    pltpu.make_async_copy(other.at[q], slot.at[1 - core], sem.at[1 - core]).start()


def arrived(slot, sem, source):
    for half in range(2):
        pltpu.make_async_copy(source.at[0], slot.at[half], sem.at[half]).wait()


def copied(source, target, sem):
    copy = pltpu.make_async_copy(source, target, sem)
    copy.start()
    copy.wait()


def add_relative(buf, q, terms):
    turn = relative(q)
    for r, term in enumerate(terms):

        @pl.when(turn == r)
        def _():
            buf[...] += term[...]


def last_device():
    return (lax.axis_index("x") == X - 1) & (lax.axis_index("z") == Z - 1)


def first_device():
    return (lax.axis_index("x") == 0) & (lax.axis_index("z") == 0)


def prepare_kernel(guess, inputs, kernels, corner, half, sem):
    two = pltpu.make_async_copy(kernels.at[0, lax.axis_index("core")], half, sem.at[1])
    two.start()

    @pl.when(last_device())
    def _():
        pltpu.make_async_copy(inputs, corner, sem.at[0]).start()

    @pl.when(jnp.logical_not(last_device()))
    def _():
        pltpu.make_async_copy(guess.at[3], corner, sem.at[0]).start()

    pltpu.make_async_copy(inputs, corner, sem.at[0]).wait()
    two.wait()


def first_kernel(head, kernels, biases, out):
    out[...] = head[...]

    def body(i, carry):
        v = out[...]
        out[...] = v + FINE * (conv(v, flat(kernels[pl.ds(i, 1)])) + biases[pl.ds(i, 1)])
        return carry

    lax.fori_loop(0, 4, body, 0)


def second_kernel(head, guess_head, kernels, biases, message, term, buf):
    @pl.when(first_device())
    def _():
        buf[...] = guess_head[...]

    @pl.when(jnp.logical_not(first_device()))
    def _():
        buf[...] = head[...]

    term[...] = buf[...]

    def body(i, carry):
        v = buf[...]
        mixed = conv(v, flat(kernels[pl.ds(i, 1)]))
        buf[...] = v + FINE * (mixed + biases[pl.ds(i, 1)])

        @pl.when(i == 0)
        def _():
            term[...] += COARSE * mixed

        return carry

    lax.fori_loop(0, 4, body, 0)
    term[...] = buf[...] - term[...]
    x = lax.axis_index("x")

    @pl.when(x == 0)
    def _():
        message[...] = buf[...]

    @pl.when(x != 0)
    def _():
        message[...] = term[...]


def third_kernel(m0, m1, m2, m3, mine, other, out, top, stack, wbuf, sem, ssem):
    x = lax.axis_index("x")
    for q in range(1, 4):
        start_lead(q, wbuf.at[q - 1], sem.at[q - 1], mine, other)
    start_lead(3, top, sem.at[3], mine, other)
    messages = (m0, m1, m2, m3)
    for r, message in enumerate(messages):
        q = lax.rem(x + r, X)

        @pl.when(q > 0)
        def _():
            pltpu.make_async_copy(message, stack.at[q - 1], ssem.at[q - 1]).start()

    out[...] = jnp.zeros((ROWS, CH), jnp.float32)
    add_relative(out, 0, messages)

    def body(q, carry):
        arrived(wbuf.at[q - 1], sem.at[q - 1], mine)
        out[...] += COARSE * conv(out[...], flat(wbuf[pl.ds(q - 1, 1)]))
        add_relative(out, q, messages)
        return carry

    lax.fori_loop(1, 4, body, 0)
    arrived(top, sem.at[3], mine)
    for q in range(3):
        pltpu.make_async_copy(m0, stack.at[q], ssem.at[q]).wait()


def start_terms(own, f1, f2, f3, stack, tbuf, sem):
    x = lax.axis_index("x")
    for r, term in enumerate((own, f1, f2, f3)):

        @pl.when(x == r)
        def _():
            pltpu.make_async_copy(term, tbuf.at[0], sem.at[0]).start()

    pltpu.make_async_copy(stack, tbuf.at[pl.ds(1, 3)], sem.at[1]).start()


def terms_arrived(own, stack, tbuf, sem):
    pltpu.make_async_copy(own, tbuf.at[0], sem.at[0]).wait()
    pltpu.make_async_copy(stack, tbuf.at[pl.ds(1, 3)], sem.at[1]).wait()


def fourth_kernel(
    hop, point, inputs, own, f1, f2, f3, stack, mine, other,
    residual, corner, start, wbuf, tbuf, sem, tsem, isem,
):
    for q in range(4):
        start_lead(q, wbuf.at[q], sem.at[q], mine, other)
    start_terms(own, f1, f2, f3, stack, tbuf, tsem)
    z = lax.axis_index("z")

    @pl.when(z == 0)
    def _():
        copied(inputs, start, isem)

    @pl.when(z != 0)
    def _():
        start[...] = hop[...]

    corner[...] = start[...]
    terms_arrived(own, stack, tbuf, tsem)

    def body(q, carry):
        arrived(wbuf.at[q], sem.at[q], mine)
        v = corner[...]
        mixed = conv(v, flat(wbuf[pl.ds(q, 1)]))
        corner[...] = v + COARSE * mixed + tbuf[pl.ds(q, 1)].reshape(ROWS, CH)
        return carry

    lax.fori_loop(0, 4, body, 0)
    x = lax.axis_index("x")

    @pl.when(x == 3)
    def _():
        residual[...] = corner[...] - point[...]

    @pl.when(x != 3)
    def _():
        residual[...] = jnp.zeros((ROWS, CH), jnp.float32)


def defect_kernel(corner, start, top, defect):
    v = start[...]
    defect[...] = corner[...] - v - TOP * conv(v, flat(top[...]))


def one_kernel(z, came, before, value, top, defect, out_before, out_value):
    @pl.when(lax.axis_index("z") == z)
    def _():
        v = came[...]
        out_before[...] = v
        out_value[...] = v + TOP * conv(v, flat(top[...])) + defect[...]


def two_kernel(
    z, came, before, value, top, defect, next_top, next_defect, out_before, out_value, ahead
):
    @pl.when(lax.axis_index("z") == z)
    def _():
        v = came[...]
        out_before[...] = v
        v = v + TOP * conv(v, flat(top[...])) + defect[...]
        out_value[...] = v
        ahead[...] = v + TOP * conv(v, flat(next_top[...])) + next_defect[...]


def last_kernel(
    w4, w7, before, value, defect, biases, own, f1, f2, f3, stack, mine, other, kernels,
    states, buf, sbuf, wbuf, tbuf, sem, tsem, ssem,
):
    x, z = lax.axis_index("x"), lax.axis_index("z")
    late = (z == 4) | (z == 6) | (z == 7)
    extra = (x == 3) & late
    for q in range(3):

        @pl.when(q < x)
        def _():
            start_lead(q, wbuf.at[q], sem.at[q], mine, other)

        start_own(kernels, q, wbuf.at[4 + q], sem.at[4 + q])

    @pl.when(extra)
    def _():
        start_lead(3, wbuf.at[3], sem.at[3], mine, other)

    start_terms(own, f1, f2, f3, stack, tbuf, tsem)

    @pl.when((z == 4) | (z == 6))
    def _():
        buf[...] = w4[...]

    @pl.when(z == 7)
    def _():
        buf[...] = w7[...]

    @pl.when(jnp.logical_not(late))
    def _():
        buf[...] = before[...]

    @pl.when((x == 3) & jnp.logical_not(late))
    def _():
        sbuf[3] = value[...]

    terms_arrived(own, stack, tbuf, tsem)

    def body(i, carry):
        slot = jnp.where(i < 0, 3, jnp.where(i < x, i, i - x + 4))
        arrived(wbuf.at[slot], sem.at[slot], mine)
        v = buf[...]
        mixed = conv(v, flat(wbuf[pl.ds(slot, 1)]))

        @pl.when(i < 0)
        def _():
            sbuf[3] = v + TOP * mixed + defect[...]

        @pl.when((i >= 0) & (i < x))
        def _():
            buf[...] = v + COARSE * mixed + tbuf[pl.ds(i, 1)].reshape(ROWS, CH)

        @pl.when((i == x) & (x < 3))
        def _():
            sbuf[3] = v + COARSE * mixed + tbuf[pl.ds(x, 1)].reshape(ROWS, CH)

        @pl.when(i >= x)
        def _():
            new = v + FINE * (mixed + biases[pl.ds(i - x, 1)])
            buf[...] = new
            sbuf[pl.ds(i - x, 1)] = new.reshape(1, ROWS, CH)
            pltpu.make_async_copy(sbuf.at[i - x], states.at[i - x], ssem.at[i - x]).start()

        @pl.when(i == x)
        def _():
            pltpu.make_async_copy(sbuf.at[3], states.at[3], ssem.at[3]).start()

        return carry

    lax.fori_loop(jnp.where(extra, -1, 0), x + 3, body, 0)
    for i in range(4):
        pltpu.make_async_copy(sbuf.at[i], states.at[i], ssem.at[i]).wait()


def call(body, name, outs, convs, args, places, scratch=(), alias=None, out_places=None, limit=16):
    specs = {
        "v": pl.BlockSpec(memory_space=pltpu.VMEM),
        "h": pl.BlockSpec(memory_space=pltpu.HBM),
    }
    out_places = out_places or "v" * len(outs)
    return pl.pallas_call(
        body,
        name=name,
        out_shape=outs,
        in_specs=[specs[p] for p in places],
        out_specs=tuple(specs[p] for p in out_places),
        scratch_shapes=scratch,
        input_output_aliases=alias or {},
        compiler_params=pltpu.CompilerParams(vmem_limit_bytes=limit << 20),
        cost_estimate=pl.CostEstimate(
            flops=convs * 2 * ROWS * CH * CH * 27,
            bytes_accessed=convs * 27 * CH * CH * 2,
            transcendentals=convs * ROWS * CH,
        ),
    )(*args)


def shards(inputs, guess_states, kernels, biases):
    state = jax.ShapeDtypeStruct((ROWS, CH), jnp.float32)
    weight = jax.ShapeDtypeStruct(WHOLE, jnp.bfloat16)
    buffer = pltpu.VMEM((ROWS, CH), jnp.float32)
    dma = pltpu.SemaphoreType.DMA
    inputs = inputs.reshape(ROWS, CH)
    guess = guess_states.reshape(4, ROWS, CH)
    kernels = kernels.reshape((4,) + WHOLE)
    barrier = lax.optimization_barrier

    def weights(slots):
        return [pltpu.VMEM((slots,) + WHOLE, jnp.bfloat16)], [dma((slots, 2))]

    def next_layer(v):
        return lax.ppermute(v, LAYER, [(i, (i + 1) % (X * Z)) for i in range(X * Z)])

    def from_ahead(v, r):
        return lax.ppermute(v, "x", [(i, (i - r) % X) for i in range(X)])

    def along_z(v, *pairs):
        return lax.ppermute(v, "z", pairs)

    guess_corner, half = call(
        prepare_kernel, "prepare",
        (state, jax.ShapeDtypeStruct((HALF, CH), jnp.bfloat16)), 0,
        (guess, inputs, kernels), "hhh", [dma((2,))], limit=63,
    )
    mine = lax.all_gather(half, "x")
    guess_head = next_layer(guess_corner)
    (point,) = call(
        first_kernel, "first", (state,), 4, (guess_head, kernels, biases), "vvv",
    )
    head = next_layer(point)
    message, term = call(
        second_kernel, "second", (state, state), 4, (head, guess_head, kernels, biases),
        "vvvv", [buffer],
    )
    m1, m2, m3 = (from_ahead(message, r) for r in (1, 2, 3))
    mine, _ = barrier((mine, message))
    other = lax.ppermute(mine, "core", [(0, 1), (1, 0)])
    group = (mine, other)
    wbuf, wsem = weights(4)
    wbuf3, _ = weights(3)
    point, top, stack = call(
        third_kernel, "third",
        (state, weight, jax.ShapeDtypeStruct((3, ROWS, CH), jnp.float32)), 3,
        (message, m1, m2, m3) + group, "vvvvhh", wbuf3 + wsem + [dma((3,))],
        out_places="vvh",
    )
    point, term = barrier((point, term))
    hop = along_z(point, *((i, i + 1) for i in range(Z - 1)))
    terms = (term, *(lax.ppermute(term, "x", [(0, i)]) for i in (1, 2, 3)), stack)
    tbuf = [pltpu.VMEM((4, ROWS, CH), jnp.float32)]
    residual, corner, start = call(
        fourth_kernel, "fourth", (state,) * 3, 4,
        (hop, point, inputs) + terms + group, "vvh" + "h" * 7,
        wbuf + tbuf + wsem + [dma((2,)), dma(())],
    )
    w2 = along_z(corner, (1, 2))
    next_top = along_z(barrier((top, corner))[0], (4, 3), (6, 5))
    (defect,) = call(defect_kernel, "defect", (state,), 1, (corner, start, top), "vvv")
    next_defect = along_z(defect, (4, 3), (6, 5))
    before, value = call(
        functools.partial(one_kernel, 2), "one", (state, state), 1,
        (w2, start, corner, top, defect), "vvvvv", alias={1: 0, 2: 1},
    )
    for z, distance in ((3, 1), (5, 2)):
        came = along_z(value if z == 3 else ahead, (z - distance, z))
        before, value, ahead = call(
            functools.partial(two_kernel, z), f"two{z}", (state,) * 3, 2,
            (came, before, value, top, defect, next_top, next_defect), "v" * 7,
            alias={1: 0, 2: 1},
        )
    w7 = along_z(ahead, (5, 7))
    w4 = along_z(value, (3, 4), (5, 6))
    wbuf7, wsem7 = weights(7)
    (states,) = call(
        last_kernel, "last", (jax.ShapeDtypeStruct((4, ROWS, CH), jnp.float32),), 6,
        (w4, w7, before, value, defect, biases) + terms + group + (kernels,),
        "v" * 6 + "h" * 8, [buffer] + tbuf + wbuf7 + tbuf + wsem7 + [dma((2,)), dma((4,))],
        out_places="h",
    )
    volume = (8, 8, 8, CH)
    return states.reshape((4, 1) + volume), residual.reshape((1, 1) + volume)


def solution(mesh):
    finer = Mesh(mesh.devices.reshape(Z, X, 4, 2), LAYER + BATCH)
    return jax.shard_map(
        shards,
        mesh=finer,
        in_specs=(P(BATCH), P(LAYER, BATCH), P(LAYER), P(LAYER)),
        out_specs=(P(LAYER, BATCH), P(LAYER, BATCH)),
        check_vma=False,
    )
```

```python
import functools

import jax
import jax.numpy as jnp
from jax import lax
from jax.experimental import pallas as pl
from jax.experimental.pallas import tpu as pltpu
from jax.sharding import Mesh
from jax.sharding import PartitionSpec as P

X, Z = 4, 8
LAYER, BATCH = ("z", "x"), ("y", "core")
ROWS, CH = 512, 128
TAPS, DEEP = 9, 384
SHARE = TAPS * DEEP // 8
WHOLE = (8, SHARE, CH)
FINE = 2.0 / 128
COARSE = 4 * FINE
TOP = 4 * COARSE


def conv(v, weights):
    t = jnp.tanh(v).reshape(64, 8, CH)
    at = lax.broadcasted_iota(jnp.int32, (64, 8, CH), 1)
    before = jnp.where(at == 0, 0.0, pltpu.roll(t, 1, 1))
    after = jnp.where(at == 7, 0.0, pltpu.roll(t, 7, 1))
    lhs = jnp.concatenate(
        [s.reshape(ROWS, CH).astype(jnp.bfloat16) for s in (before, t, after)], 1
    )
    rhs = jnp.concatenate([weights[n * DEEP : (n + 1) * DEEP] for n in range(TAPS)], 1)
    out = jnp.dot(lhs, rhs, preferred_element_type=jnp.float32)
    edge_y = jnp.zeros((8, 1, 8, CH), jnp.float32)
    edge_x = jnp.zeros((1, 8, 8, CH), jnp.float32)
    total = None
    for dx in range(3):
        for dy in range(3):
            n = dx * 3 + dy
            part = out[:, n * CH : (n + 1) * CH].reshape(8, 8, 8, CH)
            if dy == 0:
                part = jnp.concatenate([edge_y, part[:, :7]], 1)
            if dy == 2:
                part = jnp.concatenate([part[:, 1:], edge_y], 1)
            if dx == 0:
                part = jnp.concatenate([edge_x, part[:7]], 0)
            if dx == 2:
                part = jnp.concatenate([part[1:], edge_x], 0)
            total = part if total is None else total + part
    return total.reshape(ROWS, CH)


def flat(weights):
    return weights.reshape(TAPS * DEEP, CH)


def last_device():
    return (lax.axis_index("x") == X - 1) & (lax.axis_index("z") == Z - 1)


def first_device():
    return (lax.axis_index("x") == 0) & (lax.axis_index("z") == 0)


def prepare_kernel(guess, inputs, kernels, corner, share, sem):
    two = pltpu.make_async_copy(
        kernels.at[0, lax.axis_index("y") * 2 + lax.axis_index("core")], share, sem.at[1]
    )
    two.start()

    @pl.when(last_device())
    def _():
        pltpu.make_async_copy(inputs, corner, sem.at[0]).start()

    @pl.when(jnp.logical_not(last_device()))
    def _():
        pltpu.make_async_copy(guess.at[3], corner, sem.at[0]).start()

    pltpu.make_async_copy(inputs, corner, sem.at[0]).wait()
    two.wait()


def first_kernel(head, biases, kernels, out, kept, lead, sem, lsem):
    for i in range(4):
        pltpu.make_async_copy(kernels.at[i], kept.at[i], sem.at[i]).start()
    pltpu.make_async_copy(kernels.at[0], lead, lsem).start()
    out[...] = head[...]

    def body(i, carry):
        pltpu.make_async_copy(kernels.at[i], kept.at[i], sem.at[i]).wait()
        v = out[...]
        out[...] = v + FINE * (conv(v, flat(kept[pl.ds(i, 1)])) + biases[pl.ds(i, 1)])
        return carry

    lax.fori_loop(0, 4, body, 0)
    pltpu.make_async_copy(kernels.at[0], lead, lsem).wait()


def second_kernel(head, guess_head, kernels, biases, term, buf):
    @pl.when(first_device())
    def _():
        buf[...] = guess_head[...]

    @pl.when(jnp.logical_not(first_device()))
    def _():
        buf[...] = head[...]

    term[...] = buf[...]

    def body(i, carry):
        v = buf[...]
        mixed = conv(v, flat(kernels[pl.ds(i, 1)]))
        buf[...] = v + FINE * (mixed + biases[pl.ds(i, 1)])

        @pl.when(i == 0)
        def _():
            term[...] += COARSE * mixed

        return carry

    lax.fori_loop(0, 4, body, 0)
    term[...] = buf[...] - term[...]


def coarse_steps(out, stack, lead, ready=lambda q: None):
    def body(q, carry):
        ready(q)
        v = out[...]
        mixed = conv(v, flat(lead[pl.ds(q, 1)]))
        out[...] = v + COARSE * mixed + stack[pl.ds(q, 1)].reshape(ROWS, CH)
        return carry

    lax.fori_loop(0, X, body, 0)


def third_kernel(
    inputs, head, b1, b2, b3, m0, m1, m2, m3, own, others, out, stack, lead, top, part, sem
):
    x, z = lax.axis_index("x"), lax.axis_index("z")

    def copy(q, wait):
        turn = lax.rem(q - x + X, X)

        @pl.when(turn == 0)
        def _():
            one = pltpu.make_async_copy(own, lead.at[q], sem.at[q])
            one.wait() if wait else one.start()

        @pl.when(turn != 0)
        def _():
            one = pltpu.make_async_copy(others.at[:, turn - 1], lead.at[q], sem.at[q])
            one.wait() if wait else one.start()

    for q in range(X):
        copy(q, False)
    for r, term in enumerate((m0, m1, m2, m3)):
        stack[pl.ds(lax.rem(x + r, X), 1)] = term[...].reshape(1, ROWS, CH)
    for r, start in enumerate((head, b1, b2, b3)):

        @pl.when((z > 0) & (x == r))
        def _():
            out[...] = start[...]

    @pl.when(z == 0)
    def _():
        out[...] = inputs[...]

    coarse_steps(out, stack, lead, lambda q: copy(q, True))
    top[...] = lead[X - 1]
    part[...] = lead[X - 1, pl.ds(lax.axis_index("core") * 4, 4)]


def fourth_kernel(inputs, hop, point, stack, lead, residual, corner, start):
    x, z = lax.axis_index("x"), lax.axis_index("z")

    @pl.when(z == 0)
    def _():
        start[...] = inputs[...]

    @pl.when(z > 0)
    def _():
        start[...] = hop[...]

    corner[...] = start[...]
    coarse_steps(corner, stack, lead)

    @pl.when(x == X - 1)
    def _():
        residual[...] = corner[...] - point[...]

    @pl.when(x != X - 1)
    def _():
        residual[...] = jnp.zeros((ROWS, CH), jnp.float32)


def defect_kernel(corner, start, top, defect):
    v = start[...]
    defect[...] = corner[...] - v - TOP * conv(v, flat(top[...]))


def one_kernel(z, came, before, value, top, defect, out_before, out_value):
    @pl.when(lax.axis_index("z") == z)
    def _():
        v = came[...]
        out_before[...] = v
        out_value[...] = v + TOP * conv(v, flat(top[...])) + defect[...]


def two_kernel(
    z, came, before, value, top, defect, mine, other, next_defect,
    out_before, out_value, ahead, wbuf,
):
    @pl.when(lax.axis_index("z") == z)
    def _():
        v = came[...]
        out_before[...] = v
        v = v + TOP * conv(v, flat(top[...])) + defect[...]
        out_value[...] = v
        core = lax.axis_index("core")
        wbuf[pl.ds(core * 4, 4)] = mine[...]
        wbuf[pl.ds(4 - core * 4, 4)] = other[...]
        ahead[...] = v + TOP * conv(v, flat(wbuf[...])) + next_defect[...]


def last_kernel(
    w4, w7, before, value, defect, biases, stack, lead, kernels, states, buf, sbuf, sem
):
    x, z = lax.axis_index("x"), lax.axis_index("z")
    late = (z == 4) | (z == 6) | (z == 7)
    extra = (x == X - 1) & late

    @pl.when((z == 4) | (z == 6))
    def _():
        buf[...] = w4[...]

    @pl.when(z == 7)
    def _():
        buf[...] = w7[...]

    @pl.when(jnp.logical_not(late))
    def _():
        buf[...] = before[...]

    @pl.when((x == X - 1) & jnp.logical_not(late))
    def _():
        sbuf[3] = value[...]

    @pl.when(extra)
    def _():
        v = buf[...]
        sbuf[3] = v + TOP * conv(v, flat(lead[3])) + defect[...]

    def coarse(q, carry):
        v = buf[...]
        mixed = conv(v, flat(lead[pl.ds(q, 1)]))
        buf[...] = v + COARSE * mixed + stack[pl.ds(q, 1)].reshape(ROWS, CH)
        return carry

    lax.fori_loop(0, x, coarse, 0)

    def fine(i, carry):
        v = buf[...]
        mixed = conv(v, flat(kernels[pl.ds(i, 1)]))

        @pl.when((i == 0) & (x < X - 1))
        def _():
            sbuf[3] = v + COARSE * mixed + stack[pl.ds(x, 1)].reshape(ROWS, CH)

        @pl.when(i == 0)
        def _():
            pltpu.make_async_copy(sbuf.at[3], states.at[3], sem.at[3]).start()

        new = v + FINE * (mixed + biases[pl.ds(i, 1)])
        buf[...] = new
        sbuf[pl.ds(i, 1)] = new.reshape(1, ROWS, CH)
        pltpu.make_async_copy(sbuf.at[i], states.at[i], sem.at[i]).start()
        return carry

    lax.fori_loop(0, 3, fine, 0)
    for i in range(4):
        pltpu.make_async_copy(sbuf.at[i], states.at[i], sem.at[i]).wait()


def call(body, name, outs, convs, args, places, scratch=(), alias=None, out_places=None, limit=16):
    specs = {
        "v": pl.BlockSpec(memory_space=pltpu.VMEM),
        "h": pl.BlockSpec(memory_space=pltpu.HBM),
    }
    out_places = out_places or "v" * len(outs)
    return pl.pallas_call(
        body,
        name=name,
        out_shape=outs,
        in_specs=[specs[p] for p in places],
        out_specs=tuple(specs[p] for p in out_places),
        scratch_shapes=scratch,
        input_output_aliases=alias or {},
        compiler_params=pltpu.CompilerParams(vmem_limit_bytes=limit << 20),
        cost_estimate=pl.CostEstimate(
            flops=convs,
            bytes_accessed=convs,
            transcendentals=0,
        ),
    )(*args)


def shards(inputs, guess_states, kernels, biases):
    state = jax.ShapeDtypeStruct((ROWS, CH), jnp.float32)
    weight = jax.ShapeDtypeStruct(WHOLE, jnp.bfloat16)
    buffer = pltpu.VMEM((ROWS, CH), jnp.float32)
    dma = pltpu.SemaphoreType.DMA
    inputs = inputs.reshape(ROWS, CH)
    guess = guess_states.reshape(4, ROWS, CH)
    kernels = kernels.reshape((4,) + WHOLE)
    barrier = lax.optimization_barrier

    def next_layer(v):
        return lax.ppermute(v, LAYER, [(i, (i + 1) % (X * Z)) for i in range(X * Z)])

    def from_ahead(v, r):
        return lax.ppermute(v, "x", [(i, (i - r) % X) for i in range(X)])

    def along_z(v, *pairs):
        return lax.ppermute(v, "z", pairs)

    guess_corner, share = call(
        prepare_kernel, "prepare",
        (state, jax.ShapeDtypeStruct((SHARE, CH), jnp.bfloat16)), 0,
        (guess, inputs, kernels), "hhh", [dma((2,))], limit=63,
    )
    guess_head = next_layer(guess_corner)
    shares = [from_ahead(share, r) for r in (1, 2, 3)]
    guess_head, *shares = barrier((guess_head, *shares))
    others = lax.all_gather(jnp.stack(shares), BATCH)
    point, kept, own = call(
        first_kernel, "first",
        (state, jax.ShapeDtypeStruct((4,) + WHOLE, jnp.bfloat16), weight), 4,
        (guess_head, biases, kernels), "vvh", [dma((4,)), dma(())],
        out_places="vvh", limit=16,
    )
    head = next_layer(point)
    starts = [
        lax.ppermute(point, LAYER, [(X * z - 1, X * z + r) for z in range(1, Z)])
        for r in (1, 2, 3)
    ]
    (term,) = call(
        second_kernel, "second", (state,), 4, (head, guess_head, kept, biases),
        "vvvv", [buffer],
    )
    terms = [from_ahead(term, r) for r in (1, 2, 3)]
    others, *come = barrier((others, *starts, *terms))
    point, stack, lead, top, part = call(
        third_kernel, "third",
        (state, jax.ShapeDtypeStruct((X, ROWS, CH), jnp.float32))
        + tuple(jax.ShapeDtypeStruct(d + (SHARE, CH), jnp.bfloat16) for d in ((X, 8), (8,), (4,))),
        4, (inputs, head, *come[:3], term, *come[3:], own, others), "v" * 9 + "hh",
        [dma((X,))],
    )
    hop = along_z(point, *((i, i + 1) for i in range(Z - 1)))
    residual, corner, start = call(
        fourth_kernel, "fourth", (state,) * 3, 4, (inputs, hop, point, stack, lead), "vvvvv",
    )
    w2 = along_z(corner, (1, 2))
    (defect,) = call(defect_kernel, "defect", (state,), 1, (corner, start, top), "vvv")
    next_defect = along_z(defect, (4, 3), (6, 5))
    next_mine = along_z(part, (4, 3), (6, 5))
    next_mine, _ = barrier((next_mine, defect))
    next_other = lax.ppermute(next_mine, "core", [(0, 1), (1, 0)])
    before, value = call(
        functools.partial(one_kernel, 2), "one", (state, state), 1,
        (w2, start, corner, top, defect), "vvvvv", alias={1: 0, 2: 1},
    )
    for z, distance in ((3, 1), (5, 2)):
        came = along_z(value if z == 3 else ahead, (z - distance, z))
        before, value, ahead = call(
            functools.partial(two_kernel, z), f"two{z}", (state,) * 3, 2,
            (came, before, value, top, defect, next_mine, next_other, next_defect), "v" * 8,
            [pltpu.VMEM(WHOLE, jnp.bfloat16)],
            alias={1: 0, 2: 1},
        )
    w7 = along_z(ahead, (5, 7))
    w4 = along_z(value, (3, 4), (5, 6))
    (states,) = call(
        last_kernel, "last", (jax.ShapeDtypeStruct((4, ROWS, CH), jnp.float32),), 6,
        (w4, w7, before, value, defect, biases, stack, lead, kernels), "v" * 9,
        [buffer, pltpu.VMEM((4, ROWS, CH), jnp.float32), dma((4,))], out_places="h",
    )
    volume = (8, 8, 8, CH)
    return states.reshape((4, 1) + volume), residual.reshape((1, 1) + volume)


def solution(mesh):
    finer = Mesh(mesh.devices.reshape(Z, X, 4, 2), LAYER + BATCH)
    return jax.shard_map(
        shards,
        mesh=finer,
        in_specs=(P(BATCH), P(LAYER, BATCH), P(LAYER), P(LAYER)),
        out_specs=(P(LAYER, BATCH), P(LAYER, BATCH)),
        check_vma=False,
    )
```

```python
import functools

import jax
import jax.numpy as jnp
from jax import lax
from jax.experimental import pallas as pl
from jax.experimental.pallas import tpu as pltpu
from jax.sharding import Mesh
from jax.sharding import PartitionSpec as P

X, Z = 4, 8
LAYER, BATCH = ("z", "x"), ("y", "core")
ROWS, CH = 512, 128
TAPS, DEEP = 9, 384
SHARE = TAPS * DEEP // 8
WHOLE = (8, SHARE, CH)
FINE = 2.0 / 128
COARSE = 4 * FINE
TOP = 4 * COARSE


def conv(v, weights):
    t = jnp.tanh(v).reshape(64, 8, CH)
    at = lax.broadcasted_iota(jnp.int32, (64, 8, CH), 1)
    before = jnp.where(at == 0, 0.0, pltpu.roll(t, 1, 1))
    after = jnp.where(at == 7, 0.0, pltpu.roll(t, 7, 1))
    lhs = jnp.concatenate(
        [s.reshape(ROWS, CH).astype(jnp.bfloat16) for s in (before, t, after)], 1
    )
    rhs = jnp.concatenate([weights[n * DEEP : (n + 1) * DEEP] for n in range(TAPS)], 1)
    out = jnp.dot(lhs, rhs, preferred_element_type=jnp.float32)
    edge_y = jnp.zeros((8, 1, 8, CH), jnp.float32)
    edge_x = jnp.zeros((1, 8, 8, CH), jnp.float32)
    total = None
    for dx in range(3):
        for dy in range(3):
            n = dx * 3 + dy
            part = out[:, n * CH : (n + 1) * CH].reshape(8, 8, 8, CH)
            if dy == 0:
                part = jnp.concatenate([edge_y, part[:, :7]], 1)
            if dy == 2:
                part = jnp.concatenate([part[:, 1:], edge_y], 1)
            if dx == 0:
                part = jnp.concatenate([edge_x, part[:7]], 0)
            if dx == 2:
                part = jnp.concatenate([part[1:], edge_x], 0)
            total = part if total is None else total + part
    return total.reshape(ROWS, CH)


def flat(weights):
    return weights.reshape(TAPS * DEEP, CH)


def last_device():
    return (lax.axis_index("x") == X - 1) & (lax.axis_index("z") == Z - 1)


def first_device():
    return (lax.axis_index("x") == 0) & (lax.axis_index("z") == 0)


def prepare_kernel(guess, inputs, kernels, corner, share, sem):
    two = pltpu.make_async_copy(
        kernels.at[0, lax.axis_index("y") * 2 + lax.axis_index("core")], share, sem.at[1]
    )
    two.start()

    @pl.when(last_device())
    def _():
        pltpu.make_async_copy(inputs, corner, sem.at[0]).start()

    @pl.when(jnp.logical_not(last_device()))
    def _():
        pltpu.make_async_copy(guess.at[3], corner, sem.at[0]).start()

    pltpu.make_async_copy(inputs, corner, sem.at[0]).wait()
    two.wait()


def first_kernel(head, biases, kernels, out, lead, kept, sem, lsem):
    for i in range(4):
        pltpu.make_async_copy(kernels.at[i], kept.at[i], sem.at[i]).start()
    pltpu.make_async_copy(kernels.at[0], lead, lsem).start()
    out[...] = head[...]

    def body(i, carry):
        pltpu.make_async_copy(kernels.at[i], kept.at[i], sem.at[i]).wait()
        v = out[...]
        out[...] = v + FINE * (conv(v, flat(kept[pl.ds(i, 1)])) + biases[pl.ds(i, 1)])
        return carry

    lax.fori_loop(0, 4, body, 0)
    pltpu.make_async_copy(kernels.at[0], lead, lsem).wait()


def second_kernel(head, guess_head, kernels, biases, message, buf):
    @pl.when(first_device())
    def _():
        buf[...] = guess_head[...]

    @pl.when(jnp.logical_not(first_device()))
    def _():
        buf[...] = head[...]

    message[...] = buf[...]

    def body(i, carry):
        v = buf[...]
        mixed = conv(v, flat(kernels[pl.ds(i, 1)]))
        buf[...] = v + FINE * (mixed + biases[pl.ds(i, 1)])

        @pl.when(i == 0)
        def _():
            message[...] += COARSE * mixed

        return carry

    lax.fori_loop(0, 4, body, 0)
    x = lax.axis_index("x")

    @pl.when(x == 0)
    def _():
        message[...] = buf[...]

    @pl.when(x > 0)
    def _():
        message[...] = buf[...] - message[...]


def coarse_steps(out, stack, lead, first=0, ready=lambda q: None):
    def body(q, carry):
        ready(q)
        v = out[...]
        mixed = conv(v, flat(lead[pl.ds(q, 1)]))
        out[...] = v + COARSE * mixed + stack[pl.ds(q, 1)].reshape(ROWS, CH)
        return carry

    lax.fori_loop(first, X, body, 0)


def third_kernel(m0, m1, m2, m3, own, others, out, stack, lead, sem):
    x = lax.axis_index("x")

    def copy(q, wait):
        turn = lax.rem(q - x + X, X)

        @pl.when(turn == 0)
        def _():
            one = pltpu.make_async_copy(own, lead.at[q], sem.at[q])
            one.wait() if wait else one.start()

        @pl.when(turn != 0)
        def _():
            one = pltpu.make_async_copy(others.at[:, turn - 1], lead.at[q], sem.at[q])
            one.wait() if wait else one.start()

    for q in (1, 2, 3, 0):
        copy(q, False)
    for r, term in enumerate((m0, m1, m2, m3)):
        stack[pl.ds(lax.rem(x + r, X), 1)] = term[...].reshape(1, ROWS, CH)
    out[...] = stack[0]
    coarse_steps(out, stack, lead, 1, lambda q: copy(q, True))
    copy(0, True)


def head_kernel(inputs, head, b1, b2, b3, lead, stack, out, top, part, buf):
    x, z = lax.axis_index("x"), lax.axis_index("z")
    for r, start in enumerate((head, b1, b2, b3)):

        @pl.when((z > 0) & (x == r))
        def _():
            buf[...] = start[...]

    @pl.when(z == 0)
    def _():
        buf[...] = inputs[...]

    v = buf[...]
    out[0] = stack[0] - v - COARSE * conv(v, flat(lead[0]))
    out[1:] = stack[1:]
    top[...] = lead[X - 1]
    part[...] = lead[X - 1, pl.ds(lax.axis_index("core") * 4, 4)]


def fourth_kernel(inputs, hop, point, stack, lead, residual, corner, start):
    x, z = lax.axis_index("x"), lax.axis_index("z")

    @pl.when(z == 0)
    def _():
        start[...] = inputs[...]

    @pl.when(z > 0)
    def _():
        start[...] = hop[...]

    corner[...] = start[...]
    coarse_steps(corner, stack, lead)

    @pl.when(x == X - 1)
    def _():
        residual[...] = corner[...] - point[...]

    @pl.when(x != X - 1)
    def _():
        residual[...] = jnp.zeros((ROWS, CH), jnp.float32)


def defect_kernel(corner, start, top, defect):
    v = start[...]
    defect[...] = corner[...] - v - TOP * conv(v, flat(top[...]))


def one_kernel(z, came, before, value, top, defect, out_before, out_value):
    @pl.when(lax.axis_index("z") == z)
    def _():
        v = came[...]
        out_before[...] = v
        out_value[...] = v + TOP * conv(v, flat(top[...])) + defect[...]


def next_kernel(z, value, mine, other, defect, ahead, wbuf):
    @pl.when(lax.axis_index("z") == z)
    def _():
        core = lax.axis_index("core")
        wbuf[pl.ds(core * 4, 4)] = mine[...]
        wbuf[pl.ds(4 - core * 4, 4)] = other[...]
        v = value[...]
        ahead[...] = v + TOP * conv(v, flat(wbuf[...])) + defect[...]


def last_kernel(came, before, value, defect, biases, stack, lead, kernels, states, buf, sbuf, sem):
    x, z = lax.axis_index("x"), lax.axis_index("z")
    late = (z == 3) | (z == 5) | (z == 7)
    extra = (x == X - 1) & late

    @pl.when(late)
    def _():
        buf[...] = came[...]

    @pl.when(jnp.logical_not(late))
    def _():
        buf[...] = before[...]

    @pl.when((x == X - 1) & jnp.logical_not(late))
    def _():
        sbuf[3] = value[...]

    @pl.when(extra)
    def _():
        v = buf[...]
        sbuf[3] = v + TOP * conv(v, flat(lead[3])) + defect[...]

    def coarse(q, carry):
        v = buf[...]
        mixed = conv(v, flat(lead[pl.ds(q, 1)]))
        buf[...] = v + COARSE * mixed + stack[pl.ds(q, 1)].reshape(ROWS, CH)
        return carry

    lax.fori_loop(0, x, coarse, 0)

    def fine(i, carry):
        v = buf[...]
        mixed = conv(v, flat(kernels[pl.ds(i, 1)]))

        @pl.when((i == 0) & (x < X - 1))
        def _():
            sbuf[3] = v + COARSE * mixed + stack[pl.ds(x, 1)].reshape(ROWS, CH)

        @pl.when(i == 0)
        def _():
            pltpu.make_async_copy(sbuf.at[3], states.at[3], sem.at[3]).start()

        new = v + FINE * (mixed + biases[pl.ds(i, 1)])
        buf[...] = new
        sbuf[pl.ds(i, 1)] = new.reshape(1, ROWS, CH)
        pltpu.make_async_copy(sbuf.at[i], states.at[i], sem.at[i]).start()
        return carry

    lax.fori_loop(0, 3, fine, 0)
    for i in range(4):
        pltpu.make_async_copy(sbuf.at[i], states.at[i], sem.at[i]).wait()


def call(body, name, outs, convs, args, places, scratch=(), alias=None, out_places=None, limit=16):
    specs = {
        "v": pl.BlockSpec(memory_space=pltpu.VMEM),
        "h": pl.BlockSpec(memory_space=pltpu.HBM),
    }
    out_places = out_places or "v" * len(outs)
    return pl.pallas_call(
        body,
        name=name,
        out_shape=outs,
        in_specs=[specs[p] for p in places],
        out_specs=tuple(specs[p] for p in out_places),
        scratch_shapes=scratch,
        input_output_aliases=alias or {},
        compiler_params=pltpu.CompilerParams(vmem_limit_bytes=limit << 20),
        cost_estimate=pl.CostEstimate(
            flops=convs if convs != 1 else 6 * 10**9,
            bytes_accessed=convs if convs != 1 else 20 * 10**6,
            transcendentals=0,
        ),
    )(*args)


def shards(inputs, guess_states, kernels, biases):
    state = jax.ShapeDtypeStruct((ROWS, CH), jnp.float32)
    weight = jax.ShapeDtypeStruct(WHOLE, jnp.bfloat16)
    buffer = pltpu.VMEM((ROWS, CH), jnp.float32)
    dma = pltpu.SemaphoreType.DMA
    inputs = inputs.reshape(ROWS, CH)
    guess = guess_states.reshape(4, ROWS, CH)
    kernels = kernels.reshape((4,) + WHOLE)
    barrier = lax.optimization_barrier

    def next_layer(v):
        return lax.ppermute(v, LAYER, [(i, (i + 1) % (X * Z)) for i in range(X * Z)])

    def from_ahead(v, r):
        return lax.ppermute(v, "x", [(i, (i - r) % X) for i in range(X)])

    def along_z(v, *pairs):
        return lax.ppermute(v, "z", pairs)

    guess_corner, share = call(
        prepare_kernel, "prepare",
        (state, jax.ShapeDtypeStruct((SHARE, CH), jnp.bfloat16)), 0,
        (guess, inputs, kernels), "hhh", [dma((2,))], limit=63,
    )
    guess_head = next_layer(guess_corner)
    shares = [from_ahead(share, 1), None, from_ahead(share, 3)]
    shares[1] = from_ahead(shares[0], 1)
    guess_head, *shares = barrier((guess_head, *shares))
    others = lax.all_gather(jnp.stack(shares), BATCH)
    point, own = call(
        first_kernel, "first", (state, weight), 4, (guess_head, biases, kernels), "vvh",
        [pltpu.VMEM((4,) + WHOLE, jnp.bfloat16), dma((4,)), dma(())], out_places="vh", limit=48,
    )
    head = next_layer(point)
    b2, b3 = (
        lax.ppermute(point, LAYER, [(X * z - 1, X * z + r) for z in range(1, Z)]) for r in (2, 3)
    )
    (message,) = call(
        second_kernel, "second", (state,), 4,
        (head, guess_head, barrier((kernels, point))[0], biases),
        "vvvv", [buffer],
    )
    m1, m2, m3 = (from_ahead(message, r) for r in (1, 2, 3))
    b1 = lax.ppermute(b2, "x", [(2, 1)])
    others, b2, b3, m1, m2, m3 = barrier((others, b2, b3, m1, m2, m3))
    point, stack, lead = call(
        third_kernel, "third",
        (state, jax.ShapeDtypeStruct((X, ROWS, CH), jnp.float32),
         jax.ShapeDtypeStruct((X,) + WHOLE, jnp.bfloat16)),
        3, (message, m1, m2, m3, own, others), "vvvvhh", [dma((X,))],
    )
    hop = along_z(point, *((i, i + 1) for i in range(Z - 1)))
    stack, top, part = call(
        head_kernel, "head",
        (jax.ShapeDtypeStruct((X, ROWS, CH), jnp.float32), weight,
         jax.ShapeDtypeStruct((4, SHARE, CH), jnp.bfloat16)), 1,
        (inputs, head, b1, b2, b3, lead, barrier((stack, point))[0]), "v" * 7, [buffer],
    )
    next_mine = along_z(part, (3, 2), (5, 4))
    residual, corner, start = call(
        fourth_kernel, "fourth", (state,) * 3, 4, (inputs, hop, point, stack, lead), "vvvvv",
    )
    came = along_z(corner, (1, 2))
    (defect,) = call(defect_kernel, "defect", (state,), 1, (corner, start, top), "vvv")
    next_defect = along_z(defect, (3, 2), (5, 4))
    next_mine, _ = barrier((next_mine, defect))
    next_other = lax.ppermute(next_mine, "core", [(0, 1), (1, 0)])
    before, value = start, corner
    for z in (2, 4, 6):
        before, value = call(
            functools.partial(one_kernel, z), f"one{z}", (state, state), 1,
            (came, before, value, top, defect), "vvvvv", alias={1: 0, 2: 1},
        )
        if z < 6:
            (ahead,) = call(
                functools.partial(next_kernel, z), f"next{z}", (state,), 0,
                (value, next_mine, next_other, next_defect), "vvvv",
                [pltpu.VMEM(WHOLE, jnp.bfloat16)],
            )
            came = along_z(ahead, (z, z + 2))
    came = along_z(value, (2, 3), (4, 5), (6, 7))
    (states,) = call(
        last_kernel, "last", (jax.ShapeDtypeStruct((4, ROWS, CH), jnp.float32),), 6,
        (came, before, value, defect, biases, stack, lead, kernels), "v" * 8,
        [buffer, pltpu.VMEM((4, ROWS, CH), jnp.float32), dma((4,))], out_places="h",
    )
    volume = (8, 8, 8, CH)
    return states.reshape((4, 1) + volume), residual.reshape((1, 1) + volume)


def solution(mesh):
    finer = Mesh(mesh.devices.reshape(Z, X, 4, 2), LAYER + BATCH)
    return jax.shard_map(
        shards,
        mesh=finer,
        in_specs=(P(BATCH), P(LAYER, BATCH), P(LAYER), P(LAYER)),
        out_specs=(P(LAYER, BATCH), P(LAYER, BATCH)),
        check_vma=False,
    )
```

```python
import functools

import jax
import jax.numpy as jnp
from jax import lax
from jax.experimental import pallas as pl
from jax.experimental.pallas import tpu as pltpu
from jax.sharding import Mesh
from jax.sharding import PartitionSpec as P

X, Z = 4, 8
LAYER, BATCH = ("z", "x"), ("y", "core")
ROWS, CH = 512, 128
TAPS, DEEP = 9, 384
SHARE = TAPS * DEEP // 8
WHOLE = (8, SHARE, CH)
FINE = 2.0 / 128
COARSE = 4 * FINE
TOP = 4 * COARSE


def conv(v, weights):
    t = jnp.tanh(v).reshape(64, 8, CH)
    at = lax.broadcasted_iota(jnp.int32, (64, 8, CH), 1)
    before = jnp.where(at == 0, 0.0, pltpu.roll(t, 1, 1))
    after = jnp.where(at == 7, 0.0, pltpu.roll(t, 7, 1))
    lhs = jnp.concatenate(
        [s.reshape(ROWS, CH).astype(jnp.bfloat16) for s in (before, t, after)], 1
    )
    rhs = jnp.concatenate([weights[n * DEEP : (n + 1) * DEEP] for n in range(TAPS)], 1)
    out = jnp.dot(lhs, rhs, preferred_element_type=jnp.float32)
    edge_y = jnp.zeros((8, 1, 8, CH), jnp.float32)
    edge_x = jnp.zeros((1, 8, 8, CH), jnp.float32)
    total = None
    for dx in range(3):
        for dy in range(3):
            n = dx * 3 + dy
            part = out[:, n * CH : (n + 1) * CH].reshape(8, 8, 8, CH)
            if dy == 0:
                part = jnp.concatenate([edge_y, part[:, :7]], 1)
            if dy == 2:
                part = jnp.concatenate([part[:, 1:], edge_y], 1)
            if dx == 0:
                part = jnp.concatenate([edge_x, part[:7]], 0)
            if dx == 2:
                part = jnp.concatenate([part[1:], edge_x], 0)
            total = part if total is None else total + part
    return total.reshape(ROWS, CH)


def flat(weights):
    return weights.reshape(TAPS * DEEP, CH)


def last_device():
    return (lax.axis_index("x") == X - 1) & (lax.axis_index("z") == Z - 1)


def first_device():
    return (lax.axis_index("x") == 0) & (lax.axis_index("z") == 0)


def prepare_kernel(guess, inputs, kernels, corner, share, sem):
    two = pltpu.make_async_copy(
        kernels.at[0, lax.axis_index("y") * 2 + lax.axis_index("core")], share, sem.at[1]
    )
    two.start()

    @pl.when(last_device())
    def _():
        pltpu.make_async_copy(inputs, corner, sem.at[0]).start()

    @pl.when(jnp.logical_not(last_device()))
    def _():
        pltpu.make_async_copy(guess.at[3], corner, sem.at[0]).start()

    pltpu.make_async_copy(inputs, corner, sem.at[0]).wait()
    two.wait()


def first_kernel(head, biases, kernels, out, lead, kept, sem, lsem):
    for i in range(4):
        pltpu.make_async_copy(kernels.at[i], kept.at[i], sem.at[i]).start()
    pltpu.make_async_copy(kernels.at[0], lead, lsem).start()
    out[...] = head[...]

    def body(i, carry):
        pltpu.make_async_copy(kernels.at[i], kept.at[i], sem.at[i]).wait()
        v = out[...]
        out[...] = v + FINE * (conv(v, flat(kept[pl.ds(i, 1)])) + biases[pl.ds(i, 1)])
        return carry

    lax.fori_loop(0, 4, body, 0)
    pltpu.make_async_copy(kernels.at[0], lead, lsem).wait()


def second_kernel(head, guess_head, kernels, biases, message, term, buf):
    @pl.when(first_device())
    def _():
        buf[...] = guess_head[...]

    @pl.when(jnp.logical_not(first_device()))
    def _():
        buf[...] = head[...]

    term[...] = buf[...]

    def body(i, carry):
        v = buf[...]
        mixed = conv(v, flat(kernels[pl.ds(i, 1)]))
        buf[...] = v + FINE * (mixed + biases[pl.ds(i, 1)])

        @pl.when(i == 0)
        def _():
            term[...] += COARSE * mixed

        return carry

    lax.fori_loop(0, 4, body, 0)
    term[...] = buf[...] - term[...]
    x = lax.axis_index("x")

    @pl.when(x == 0)
    def _():
        message[...] = buf[...]

    @pl.when(x > 0)
    def _():
        message[...] = term[...]


def coarse_steps(out, stack, lead, first=0, ready=lambda q: None):
    def body(q, carry):
        ready(q)
        v = out[...]
        mixed = conv(v, flat(lead[pl.ds(q, 1)]))
        out[...] = v + COARSE * mixed + stack[pl.ds(q, 1)].reshape(ROWS, CH)
        return carry

    lax.fori_loop(first, X, body, 0)


def third_kernel(m0, m1, m2, m3, own, others, out, stack, lead, top, part, sem):
    x = lax.axis_index("x")

    def copy(q, wait):
        turn = lax.rem(q - x + X, X)

        @pl.when(turn == 0)
        def _():
            one = pltpu.make_async_copy(own, lead.at[q], sem.at[q])
            one.wait() if wait else one.start()

        @pl.when(turn != 0)
        def _():
            one = pltpu.make_async_copy(others.at[:, turn - 1], lead.at[q], sem.at[q])
            one.wait() if wait else one.start()

    for q in (1, 2, 3, 0):
        copy(q, False)
    for r, term in enumerate((m0, m1, m2, m3)):
        stack[pl.ds(lax.rem(x + r, X), 1)] = term[...].reshape(1, ROWS, CH)
    out[...] = stack[0]
    coarse_steps(out, stack, lead, 1, lambda q: copy(q, True))
    copy(0, True)
    top[...] = lead[X - 1]
    part[...] = lead[X - 1, pl.ds(lax.axis_index("core") * 4, 4)]


def fourth_kernel(
    inputs, hop, point, term, f1, f2, f3, stack, lead, residual, corner, start, out_stack
):
    x, z = lax.axis_index("x"), lax.axis_index("z")
    out_stack[1:] = stack[1:]
    for r, first in enumerate((term, f1, f2, f3)):

        @pl.when(x == r)
        def _():
            out_stack[0] = first[...]


    @pl.when(z == 0)
    def _():
        start[...] = inputs[...]

    @pl.when(z > 0)
    def _():
        start[...] = hop[...]

    corner[...] = start[...]
    coarse_steps(corner, out_stack, lead)

    @pl.when(x == X - 1)
    def _():
        residual[...] = corner[...] - point[...]

    @pl.when(x != X - 1)
    def _():
        residual[...] = jnp.zeros((ROWS, CH), jnp.float32)


def defect_kernel(corner, start, top, defect):
    v = start[...]
    defect[...] = corner[...] - v - TOP * conv(v, flat(top[...]))


def one_kernel(z, came, before, value, top, defect, out_before, out_value):
    @pl.when(lax.axis_index("z") == z)
    def _():
        v = came[...]
        out_before[...] = v
        out_value[...] = v + TOP * conv(v, flat(top[...])) + defect[...]


def next_kernel(z, value, mine, other, defect, ahead, wbuf):
    @pl.when(lax.axis_index("z") == z)
    def _():
        core = lax.axis_index("core")
        wbuf[pl.ds(core * 4, 4)] = mine[...]
        wbuf[pl.ds(4 - core * 4, 4)] = other[...]
        v = value[...]
        ahead[...] = v + TOP * conv(v, flat(wbuf[...])) + defect[...]


def last_kernel(came, before, value, defect, biases, stack, lead, kernels, states, buf, sbuf, sem):
    x, z = lax.axis_index("x"), lax.axis_index("z")
    late = (z == 3) | (z == 5) | (z == 7)
    extra = (x == X - 1) & late

    @pl.when(late)
    def _():
        buf[...] = came[...]

    @pl.when(jnp.logical_not(late))
    def _():
        buf[...] = before[...]

    @pl.when((x == X - 1) & jnp.logical_not(late))
    def _():
        sbuf[3] = value[...]

    @pl.when(extra)
    def _():
        v = buf[...]
        sbuf[3] = v + TOP * conv(v, flat(lead[3])) + defect[...]

    def coarse(q, carry):
        v = buf[...]
        mixed = conv(v, flat(lead[pl.ds(q, 1)]))
        buf[...] = v + COARSE * mixed + stack[pl.ds(q, 1)].reshape(ROWS, CH)
        return carry

    lax.fori_loop(0, x, coarse, 0)

    def fine(i, carry):
        v = buf[...]
        mixed = conv(v, flat(kernels[pl.ds(i, 1)]))

        @pl.when((i == 0) & (x < X - 1))
        def _():
            sbuf[3] = v + COARSE * mixed + stack[pl.ds(x, 1)].reshape(ROWS, CH)

        @pl.when(i == 0)
        def _():
            pltpu.make_async_copy(sbuf.at[3], states.at[3], sem.at[3]).start()

        new = v + FINE * (mixed + biases[pl.ds(i, 1)])
        buf[...] = new
        sbuf[pl.ds(i, 1)] = new.reshape(1, ROWS, CH)
        pltpu.make_async_copy(sbuf.at[i], states.at[i], sem.at[i]).start()
        return carry

    lax.fori_loop(0, 3, fine, 0)
    for i in range(4):
        pltpu.make_async_copy(sbuf.at[i], states.at[i], sem.at[i]).wait()


def call(body, name, outs, convs, args, places, scratch=(), alias=None, out_places=None, limit=16):
    specs = {
        "v": pl.BlockSpec(memory_space=pltpu.VMEM),
        "h": pl.BlockSpec(memory_space=pltpu.HBM),
    }
    out_places = out_places or "v" * len(outs)
    return pl.pallas_call(
        body,
        name=name,
        out_shape=outs,
        in_specs=[specs[p] for p in places],
        out_specs=tuple(specs[p] for p in out_places),
        scratch_shapes=scratch,
        input_output_aliases=alias or {},
        compiler_params=pltpu.CompilerParams(vmem_limit_bytes=limit << 20),
        cost_estimate=pl.CostEstimate(
            flops=convs if convs != 1 else 6 * 10**9,
            bytes_accessed=convs if convs != 1 else 20 * 10**6,
            transcendentals=0,
        ),
    )(*args)


def shards(inputs, guess_states, kernels, biases):
    state = jax.ShapeDtypeStruct((ROWS, CH), jnp.float32)
    weight = jax.ShapeDtypeStruct(WHOLE, jnp.bfloat16)
    buffer = pltpu.VMEM((ROWS, CH), jnp.float32)
    dma = pltpu.SemaphoreType.DMA
    inputs = inputs.reshape(ROWS, CH)
    guess = guess_states.reshape(4, ROWS, CH)
    kernels = kernels.reshape((4,) + WHOLE)
    barrier = lax.optimization_barrier

    def next_layer(v):
        return lax.ppermute(v, LAYER, [(i, (i + 1) % (X * Z)) for i in range(X * Z)])

    def from_ahead(v, r):
        return lax.ppermute(v, "x", [(i, (i - r) % X) for i in range(X)])

    def along_z(v, *pairs):
        return lax.ppermute(v, "z", pairs)

    guess_corner, share = call(
        prepare_kernel, "prepare",
        (state, jax.ShapeDtypeStruct((SHARE, CH), jnp.bfloat16)), 0,
        (guess, inputs, kernels), "hhh", [dma((2,))], limit=63,
    )
    guess_head = next_layer(guess_corner)
    shares = [from_ahead(share, 1), None, from_ahead(share, 3)]
    shares[1] = from_ahead(shares[0], 1)
    guess_head, *shares = barrier((guess_head, *shares))
    others = lax.all_gather(jnp.stack(shares), BATCH)
    point, own = call(
        first_kernel, "first", (state, weight), 4, (guess_head, biases, kernels), "vvh",
        [pltpu.VMEM((4,) + WHOLE, jnp.bfloat16), dma((4,)), dma(())], out_places="vh", limit=48,
    )
    head = next_layer(point)
    message, term = call(
        second_kernel, "second", (state, state), 4,
        (head, guess_head, barrier((kernels, point))[0], biases),
        "vvvv", [buffer],
    )
    m1, m2, m3 = (from_ahead(message, r) for r in (1, 2, 3))
    others, term, m1, m2, m3 = barrier((others, term, m1, m2, m3))
    f1, f3 = (lax.ppermute(term, "x", [(0, r)]) for r in (1, 3))
    stacked = jax.ShapeDtypeStruct((X, ROWS, CH), jnp.float32)
    point, stack, lead, top, part = call(
        third_kernel, "third",
        (state, stacked, jax.ShapeDtypeStruct((X,) + WHOLE, jnp.bfloat16), weight,
         jax.ShapeDtypeStruct((4, SHARE, CH), jnp.bfloat16)),
        3, (message, m1, m2, m3, own, others), "vvvvhh", [dma((X,))],
    )
    hop = along_z(point, *((i, i + 1) for i in range(Z - 1)))
    f2 = lax.ppermute(f1, "x", [(1, 2)])
    next_mine = along_z(part, (3, 2), (5, 4))
    residual, corner, start, stack = call(
        fourth_kernel, "fourth", (state,) * 3 + (stacked,), 1,
        (inputs, hop, point, term, f1, f2, f3, stack, lead), "v" * 9,
    )
    came = along_z(corner, (1, 2))
    (defect,) = call(defect_kernel, "defect", (state,), 1, (corner, start, top), "vvv")
    next_defect = {2: along_z(defect, (3, 2)), 4: along_z(defect, (5, 4))}
    next_mine, _ = barrier((next_mine, defect))
    next_other = lax.ppermute(next_mine, "core", [(0, 1), (1, 0)])
    before, value = start, corner
    for z in (2, 4, 6):
        before, value = call(
            functools.partial(one_kernel, z), f"one{z}", (state, state), 1,
            (came, before, value, top, defect), "vvvvv", alias={1: 0, 2: 1},
        )
        if z < 6:
            (ahead,) = call(
                functools.partial(next_kernel, z), f"next{z}", (state,), 0,
                (value, next_mine, next_other, next_defect[z]), "vvvv",
                [pltpu.VMEM(WHOLE, jnp.bfloat16)],
            )
            came = along_z(ahead, (z, z + 2))
    came = along_z(value, (2, 3), (4, 5), (6, 7))
    (states,) = call(
        last_kernel, "last", (jax.ShapeDtypeStruct((4, ROWS, CH), jnp.float32),), 6,
        (came, before, value, defect, biases, stack, lead, kernels), "v" * 8,
        [buffer, pltpu.VMEM((4, ROWS, CH), jnp.float32), dma((4,))], out_places="h",
    )
    volume = (8, 8, 8, CH)
    return states.reshape((4, 1) + volume), residual.reshape((1, 1) + volume)


def solution(mesh):
    finer = Mesh(mesh.devices.reshape(Z, X, 4, 2), LAYER + BATCH)
    return jax.shard_map(
        shards,
        mesh=finer,
        in_specs=(P(BATCH), P(LAYER, BATCH), P(LAYER), P(LAYER)),
        out_specs=(P(LAYER, BATCH), P(LAYER, BATCH)),
        check_vma=False,
    )
```

```python
import functools

import jax
import jax.numpy as jnp
from jax import lax
from jax.experimental import pallas as pl
from jax.experimental.pallas import tpu as pltpu
from jax.sharding import Mesh
from jax.sharding import PartitionSpec as P

X, Z = 4, 8
LAYER, BATCH = ("z", "x"), ("y", "core")
ROWS, CH = 512, 128
TAPS, DEEP = 9, 384
SHARE = TAPS * DEEP // 8
WHOLE = (8, SHARE, CH)
FINE = 2.0 / 128
COARSE = 4 * FINE
TOP = 4 * COARSE


def conv(v, weights):
    t = jnp.tanh(v).reshape(64, 8, CH)
    at = lax.broadcasted_iota(jnp.int32, (64, 8, CH), 1)
    before = jnp.where(at == 0, 0.0, pltpu.roll(t, 1, 1))
    after = jnp.where(at == 7, 0.0, pltpu.roll(t, 7, 1))
    lhs = jnp.concatenate(
        [s.reshape(ROWS, CH).astype(jnp.bfloat16) for s in (before, t, after)], 1
    )
    rhs = jnp.concatenate([weights[n * DEEP : (n + 1) * DEEP] for n in range(TAPS)], 1)
    out = jnp.dot(lhs, rhs, preferred_element_type=jnp.float32)
    edge_y = jnp.zeros((8, 1, 8, CH), jnp.float32)
    edge_x = jnp.zeros((1, 8, 8, CH), jnp.float32)
    total = None
    for dx in range(3):
        for dy in range(3):
            n = dx * 3 + dy
            part = out[:, n * CH : (n + 1) * CH].reshape(8, 8, 8, CH)
            if dy == 0:
                part = jnp.concatenate([edge_y, part[:, :7]], 1)
            if dy == 2:
                part = jnp.concatenate([part[:, 1:], edge_y], 1)
            if dx == 0:
                part = jnp.concatenate([edge_x, part[:7]], 0)
            if dx == 2:
                part = jnp.concatenate([part[1:], edge_x], 0)
            total = part if total is None else total + part
    return total.reshape(ROWS, CH)


def flat(weights):
    return weights.reshape(TAPS * DEEP, CH)


def last_device():
    return (lax.axis_index("x") == X - 1) & (lax.axis_index("z") == Z - 1)


def first_device():
    return (lax.axis_index("x") == 0) & (lax.axis_index("z") == 0)


def prepare_kernel(guess, inputs, kernels, corner, share, sem):
    two = pltpu.make_async_copy(
        kernels.at[0, lax.axis_index("y") * 2 + lax.axis_index("core")], share, sem.at[1]
    )
    two.start()

    @pl.when(last_device())
    def _():
        pltpu.make_async_copy(inputs, corner, sem.at[0]).start()

    @pl.when(jnp.logical_not(last_device()))
    def _():
        pltpu.make_async_copy(guess.at[3], corner, sem.at[0]).start()

    pltpu.make_async_copy(inputs, corner, sem.at[0]).wait()
    two.wait()


def load_kernel(kernels, kept, sem):
    copy = pltpu.make_async_copy(kernels, kept, sem)
    copy.start()
    copy.wait()


def first_kernel(head, kernels, biases, out):
    out[...] = head[...]

    def body(i, carry):
        v = out[...]
        out[...] = v + FINE * (conv(v, flat(kernels[pl.ds(i, 1)])) + biases[pl.ds(i, 1)])
        return carry

    lax.fori_loop(0, 4, body, 0)


def second_kernel(head, guess_head, kernels, biases, message, term, buf):
    @pl.when(first_device())
    def _():
        buf[...] = guess_head[...]

    @pl.when(jnp.logical_not(first_device()))
    def _():
        buf[...] = head[...]

    term[...] = buf[...]

    def body(i, carry):
        v = buf[...]
        mixed = conv(v, flat(kernels[pl.ds(i, 1)]))
        buf[...] = v + FINE * (mixed + biases[pl.ds(i, 1)])

        @pl.when(i == 0)
        def _():
            term[...] += COARSE * mixed

        return carry

    lax.fori_loop(0, 4, body, 0)
    term[...] = buf[...] - term[...]
    x = lax.axis_index("x")

    @pl.when(x == 0)
    def _():
        message[...] = buf[...]

    @pl.when(x > 0)
    def _():
        message[...] = term[...]


def coarse_steps(out, stack, lead, first=0, ready=lambda q: None):
    def body(q, carry):
        ready(q)
        v = out[...]
        mixed = conv(v, flat(lead[pl.ds(q, 1)]))
        out[...] = v + COARSE * mixed + stack[pl.ds(q, 1)].reshape(ROWS, CH)
        return carry

    lax.fori_loop(first, X, body, 0)


def third_kernel(
    m0, m1, m2, m3, kernels, p0, p1, p2, p3, o0, o1, o2, o3, out, stack, lead, top, part
):
    x, y, core = lax.axis_index("x"), lax.axis_index("y"), lax.axis_index("core")
    lead[pl.ds(x, 1)] = kernels[pl.ds(0, 1)]
    for offset, mine, other in ((0, p0, o0), (3, p1, o1), (1, p2, o2), (2, p3, o3)):
        at = lax.rem(y + offset, 4) * 2
        for r in range(1, X):
            q = pl.ds(lax.rem(x + r, X), 1)
            lead[q, pl.ds(at + core, 1)] = mine[r - 1].reshape(1, 1, SHARE, CH)
            lead[q, pl.ds(at + 1 - core, 1)] = other[r - 1].reshape(1, 1, SHARE, CH)
    for r, term in enumerate((m0, m1, m2, m3)):
        stack[pl.ds(lax.rem(x + r, X), 1)] = term[...].reshape(1, ROWS, CH)
    out[...] = stack[0]
    coarse_steps(out, stack, lead, 1)
    top[...] = lead[X - 1]
    part[...] = lead[X - 1, pl.ds(core * 4, 4)]


def fourth_kernel(
    inputs, hop, point, term, f1, f2, f3, stack, lead, residual, corner, start, out_stack
):
    x, z = lax.axis_index("x"), lax.axis_index("z")
    out_stack[1:] = stack[1:]
    for r, first in enumerate((term, f1, f2, f3)):

        @pl.when(x == r)
        def _():
            out_stack[0] = first[...]


    @pl.when(z == 0)
    def _():
        start[...] = inputs[...]

    @pl.when(z > 0)
    def _():
        start[...] = hop[...]

    corner[...] = start[...]
    coarse_steps(corner, out_stack, lead)

    @pl.when(x == X - 1)
    def _():
        residual[...] = corner[...] - point[...]

    @pl.when(x != X - 1)
    def _():
        residual[...] = jnp.zeros((ROWS, CH), jnp.float32)


def defect_kernel(corner, start, top, defect):
    v = start[...]
    defect[...] = corner[...] - v - TOP * conv(v, flat(top[...]))


def one_kernel(z, came, before, value, top, defect, out_before, out_value):
    @pl.when(lax.axis_index("z") == z)
    def _():
        v = came[...]
        out_before[...] = v
        out_value[...] = v + TOP * conv(v, flat(top[...])) + defect[...]


def next_kernel(z, value, mine, other, defect, ahead, wbuf):
    @pl.when(lax.axis_index("z") == z)
    def _():
        core = lax.axis_index("core")
        wbuf[pl.ds(core * 4, 4)] = mine[...]
        wbuf[pl.ds(4 - core * 4, 4)] = other[...]
        v = value[...]
        ahead[...] = v + TOP * conv(v, flat(wbuf[...])) + defect[...]


def last_kernel(came, before, value, defect, biases, stack, lead, kernels, states, buf, sbuf, sem):
    x, z = lax.axis_index("x"), lax.axis_index("z")
    late = (z == 3) | (z == 5) | (z == 7)
    extra = (x == X - 1) & late

    @pl.when(late)
    def _():
        buf[...] = came[...]

    @pl.when(jnp.logical_not(late))
    def _():
        buf[...] = before[...]

    @pl.when((x == X - 1) & jnp.logical_not(late))
    def _():
        sbuf[3] = value[...]

    @pl.when(extra)
    def _():
        v = buf[...]
        sbuf[3] = v + TOP * conv(v, flat(lead[3])) + defect[...]

    def coarse(q, carry):
        v = buf[...]
        mixed = conv(v, flat(lead[pl.ds(q, 1)]))
        buf[...] = v + COARSE * mixed + stack[pl.ds(q, 1)].reshape(ROWS, CH)
        return carry

    lax.fori_loop(0, x, coarse, 0)

    def fine(i, carry):
        v = buf[...]
        mixed = conv(v, flat(kernels[pl.ds(i, 1)]))

        @pl.when((i == 0) & (x < X - 1))
        def _():
            sbuf[3] = v + COARSE * mixed + stack[pl.ds(x, 1)].reshape(ROWS, CH)

        @pl.when(i == 0)
        def _():
            pltpu.make_async_copy(sbuf.at[3], states.at[3], sem.at[3]).start()

        new = v + FINE * (mixed + biases[pl.ds(i, 1)])
        buf[...] = new
        sbuf[pl.ds(i, 1)] = new.reshape(1, ROWS, CH)
        pltpu.make_async_copy(sbuf.at[i], states.at[i], sem.at[i]).start()
        return carry

    lax.fori_loop(0, 3, fine, 0)
    for i in range(4):
        pltpu.make_async_copy(sbuf.at[i], states.at[i], sem.at[i]).wait()


def call(body, name, outs, convs, args, places, scratch=(), alias=None, out_places=None, limit=16):
    specs = {
        "v": pl.BlockSpec(memory_space=pltpu.VMEM),
        "h": pl.BlockSpec(memory_space=pltpu.HBM),
    }
    out_places = out_places or "v" * len(outs)
    return pl.pallas_call(
        body,
        name=name,
        out_shape=outs,
        in_specs=[specs[p] for p in places],
        out_specs=tuple(specs[p] for p in out_places),
        scratch_shapes=scratch,
        input_output_aliases=alias or {},
        compiler_params=pltpu.CompilerParams(vmem_limit_bytes=limit << 20),
        cost_estimate=pl.CostEstimate(
            flops=convs if convs != 1 else 6 * 10**9,
            bytes_accessed=convs if convs != 1 else 20 * 10**6,
            transcendentals=0,
        ),
    )(*args)


def shards(inputs, guess_states, kernels, biases):
    state = jax.ShapeDtypeStruct((ROWS, CH), jnp.float32)
    weight = jax.ShapeDtypeStruct(WHOLE, jnp.bfloat16)
    buffer = pltpu.VMEM((ROWS, CH), jnp.float32)
    dma = pltpu.SemaphoreType.DMA
    inputs = inputs.reshape(ROWS, CH)
    guess = guess_states.reshape(4, ROWS, CH)
    kernels = kernels.reshape((4,) + WHOLE)
    barrier = lax.optimization_barrier

    def next_layer(v):
        return lax.ppermute(v, LAYER, [(i, (i + 1) % (X * Z)) for i in range(X * Z)])

    def from_ahead(v, r):
        return lax.ppermute(v, "x", [(i, (i - r) % X) for i in range(X)])

    def along_z(v, *pairs):
        return lax.ppermute(v, "z", pairs)

    guess_corner, share = call(
        prepare_kernel, "prepare",
        (state, jax.ShapeDtypeStruct((SHARE, CH), jnp.bfloat16)), 0,
        (guess, inputs, kernels), "hhh", [dma((2,))], limit=63,
    )
    guess_head = next_layer(guess_corner)
    shares = [from_ahead(share, 1), None, from_ahead(share, 3)]
    shares[1] = from_ahead(shares[0], 1)
    (kept,) = call(
        load_kernel, "load", (jax.ShapeDtypeStruct((4,) + WHOLE, jnp.bfloat16),), 0,
        (barrier((kernels, guess_corner))[0],), "h", [dma(())],
    )
    (point,) = call(
        first_kernel, "first", (state,), 4, (guess_head, kept, biases), "vvv",
    )
    head = next_layer(point)
    first_piece = jnp.stack(barrier((point, *shares))[1:])
    pieces = [first_piece] + [
        lax.ppermute(first_piece, "y", [(i, (i + r) % 4) for i in range(4)]) for r in (1, 3, 2)
    ]
    message, term = call(
        second_kernel, "second", (state, state), 4,
        (head, guess_head, kept, biases),
        "vvvv", [buffer],
    )
    m2, m3, m1 = (from_ahead(message, r) for r in (2, 3, 1))
    pieces, m2, m3 = barrier((pieces, m2, m3))
    pieces += [lax.ppermute(p, "core", [(0, 1), (1, 0)]) for p in pieces]
    term, m1, m2, m3 = barrier((term, m1, m2, m3))
    f1, f3 = (lax.ppermute(term, "x", [(0, r)]) for r in (1, 3))
    stacked = jax.ShapeDtypeStruct((X, ROWS, CH), jnp.float32)
    point, stack, lead, top, part = call(
        third_kernel, "third",
        (state, stacked, jax.ShapeDtypeStruct((X,) + WHOLE, jnp.bfloat16), weight,
         jax.ShapeDtypeStruct((4, SHARE, CH), jnp.bfloat16)),
        3, (message, m1, m2, m3, kept, *pieces), "v" * 13,
    )
    hop = along_z(point, *((i, i + 1) for i in range(Z - 1)))
    f2 = lax.ppermute(f1, "x", [(1, 2)])
    next_mine = along_z(part, (3, 2), (5, 4))
    residual, corner, start, stack = call(
        fourth_kernel, "fourth", (state,) * 3 + (stacked,), 1,
        (inputs, hop, point, term, f1, f2, f3, stack, lead), "v" * 9,
    )
    came = along_z(corner, (1, 2))
    (defect,) = call(defect_kernel, "defect", (state,), 1, (corner, start, top), "vvv")
    next_defect = {2: along_z(defect, (3, 2)), 4: along_z(defect, (5, 4))}
    next_mine, _ = barrier((next_mine, defect))
    next_other = lax.ppermute(next_mine, "core", [(0, 1), (1, 0)])
    before, value = start, corner
    for z in (2, 4, 6):
        before, value = call(
            functools.partial(one_kernel, z), f"one{z}", (state, state), 1,
            (came, before, value, top, defect), "vvvvv", alias={1: 0, 2: 1},
        )
        if z < 6:
            (ahead,) = call(
                functools.partial(next_kernel, z), f"next{z}", (state,), 0,
                (value, next_mine, next_other, next_defect[z]), "vvvv",
                [pltpu.VMEM(WHOLE, jnp.bfloat16)],
            )
            came = along_z(ahead, (z, z + 2))
    came = along_z(value, (2, 3), (4, 5), (6, 7))
    (states,) = call(
        last_kernel, "last", (jax.ShapeDtypeStruct((4, ROWS, CH), jnp.float32),), 6,
        (came, before, value, defect, biases, stack, lead, kept), "v" * 8,
        [buffer, pltpu.VMEM((4, ROWS, CH), jnp.float32), dma((4,))], out_places="h",
    )
    volume = (8, 8, 8, CH)
    return states.reshape((4, 1) + volume), residual.reshape((1, 1) + volume)


def solution(mesh):
    finer = Mesh(mesh.devices.reshape(Z, X, 4, 2), LAYER + BATCH)
    return jax.shard_map(
        shards,
        mesh=finer,
        in_specs=(P(BATCH), P(LAYER, BATCH), P(LAYER), P(LAYER)),
        out_specs=(P(LAYER, BATCH), P(LAYER, BATCH)),
        check_vma=False,
    )
```

```python
import functools

import jax
import jax.numpy as jnp
from jax import lax
from jax.experimental import pallas as pl
from jax.experimental.pallas import tpu as pltpu
from jax.sharding import Mesh
from jax.sharding import PartitionSpec as P

X, Z = 4, 8
LAYER, BATCH = ("z", "x"), ("y", "core")
ROWS, CH = 512, 128
TAPS, DEEP = 9, 384
SHARE = TAPS * DEEP // 8
WHOLE = (8, SHARE, CH)
FINE = 2.0 / 128
COARSE = 4 * FINE
TOP = 4 * COARSE


def conv(v, weights):
    t = jnp.tanh(v).reshape(64, 8, CH)
    at = lax.broadcasted_iota(jnp.int32, (64, 8, CH), 1)
    before = jnp.where(at == 0, 0.0, pltpu.roll(t, 1, 1))
    after = jnp.where(at == 7, 0.0, pltpu.roll(t, 7, 1))
    lhs = jnp.concatenate(
        [s.reshape(ROWS, CH).astype(jnp.bfloat16) for s in (before, t, after)], 1
    )
    rhs = jnp.concatenate([weights[n * DEEP : (n + 1) * DEEP] for n in range(TAPS)], 1)
    out = jnp.dot(lhs, rhs, preferred_element_type=jnp.float32)
    edge_y = jnp.zeros((8, 1, 8, CH), jnp.float32)
    edge_x = jnp.zeros((1, 8, 8, CH), jnp.float32)
    total = None
    for dx in range(3):
        for dy in range(3):
            n = dx * 3 + dy
            part = out[:, n * CH : (n + 1) * CH].reshape(8, 8, 8, CH)
            if dy == 0:
                part = jnp.concatenate([edge_y, part[:, :7]], 1)
            if dy == 2:
                part = jnp.concatenate([part[:, 1:], edge_y], 1)
            if dx == 0:
                part = jnp.concatenate([edge_x, part[:7]], 0)
            if dx == 2:
                part = jnp.concatenate([part[1:], edge_x], 0)
            total = part if total is None else total + part
    return total.reshape(ROWS, CH)


def flat(weights):
    return weights.reshape(TAPS * DEEP, CH)


def last_device():
    return (lax.axis_index("x") == X - 1) & (lax.axis_index("z") == Z - 1)


def first_device():
    return (lax.axis_index("x") == 0) & (lax.axis_index("z") == 0)


def prepare_kernel(guess, inputs, kernels, corner, share, sem):
    two = pltpu.make_async_copy(
        kernels.at[0, lax.axis_index("y") * 2 + lax.axis_index("core")], share, sem.at[1]
    )
    two.start()

    @pl.when(last_device())
    def _():
        pltpu.make_async_copy(inputs, corner, sem.at[0]).start()

    @pl.when(jnp.logical_not(last_device()))
    def _():
        pltpu.make_async_copy(guess.at[3], corner, sem.at[0]).start()

    pltpu.make_async_copy(inputs, corner, sem.at[0]).wait()
    two.wait()


def load_kernel(kernels, kept, sem):
    copy = pltpu.make_async_copy(kernels, kept, sem)
    copy.start()
    copy.wait()


def first_kernel(head, kernels, biases, out):
    out[...] = head[...]

    def body(i, carry):
        v = out[...]
        out[...] = v + FINE * (conv(v, flat(kernels[pl.ds(i, 1)])) + biases[pl.ds(i, 1)])
        return carry

    lax.fori_loop(0, 4, body, 0)


def second_kernel(head, guess_head, kernels, biases, message, term, buf):
    @pl.when(first_device())
    def _():
        buf[...] = guess_head[...]

    @pl.when(jnp.logical_not(first_device()))
    def _():
        buf[...] = head[...]

    term[...] = buf[...]

    def body(i, carry):
        v = buf[...]
        mixed = conv(v, flat(kernels[pl.ds(i, 1)]))
        buf[...] = v + FINE * (mixed + biases[pl.ds(i, 1)])

        @pl.when(i == 0)
        def _():
            term[...] += COARSE * mixed

        return carry

    lax.fori_loop(0, 4, body, 0)
    term[...] = buf[...] - term[...]
    x = lax.axis_index("x")

    @pl.when(x == 0)
    def _():
        message[...] = buf[...]

    @pl.when(x > 0)
    def _():
        message[...] = term[...]


def coarse_steps(out, stack, lead, first=0, ready=lambda q: None):
    def body(q, carry):
        ready(q)
        v = out[...]
        mixed = conv(v, flat(lead[pl.ds(q, 1)]))
        out[...] = v + COARSE * mixed + stack[pl.ds(q, 1)].reshape(ROWS, CH)
        return carry

    lax.fori_loop(first, X, body, 0)


def third_kernel(
    m0, m1, m2, m3, kernels, p0, p1, p2, p3, o0, o1, o2, o3, out, stack, lead, top, part
):
    x, y, core = lax.axis_index("x"), lax.axis_index("y"), lax.axis_index("core")
    lead[pl.ds(x, 1)] = kernels[pl.ds(0, 1)]
    for offset, mine, other in ((0, p0, o0), (3, p1, o1), (1, p2, o2), (2, p3, o3)):
        at = lax.rem(y + offset, 4) * 2
        for r in range(1, X):
            q = pl.ds(lax.rem(x + r, X), 1)
            lead[q, pl.ds(at + core, 1)] = mine[r - 1].reshape(1, 1, SHARE, CH)
            lead[q, pl.ds(at + 1 - core, 1)] = other[r - 1].reshape(1, 1, SHARE, CH)
    for r, term in enumerate((m0, m1, m2, m3)):
        stack[pl.ds(lax.rem(x + r, X), 1)] = term[...].reshape(1, ROWS, CH)
    out[...] = stack[0]
    coarse_steps(out, stack, lead, 1)
    top[...] = lead[X - 1]
    part[...] = lead[X - 1, pl.ds(core * 4, 4)]


def fourth_kernel(
    inputs, hop, point, term, f1, f2, f3, stack, lead, residual, corner, start, out_stack
):
    x, z = lax.axis_index("x"), lax.axis_index("z")
    out_stack[1:] = stack[1:]
    for r, first in enumerate((term, f1, f2, f3)):

        @pl.when(x == r)
        def _():
            out_stack[0] = first[...]


    @pl.when(z == 0)
    def _():
        start[...] = inputs[...]

    @pl.when(z > 0)
    def _():
        start[...] = hop[...]

    corner[...] = start[...]
    coarse_steps(corner, out_stack, lead)

    @pl.when(x == X - 1)
    def _():
        residual[...] = corner[...] - point[...]

    @pl.when(x != X - 1)
    def _():
        residual[...] = jnp.zeros((ROWS, CH), jnp.float32)


def defect_kernel(corner, start, top, defect):
    v = start[...]
    defect[...] = corner[...] - v - TOP * conv(v, flat(top[...]))


def one_kernel(z, came, before, value, top, defect, out_before, out_value):
    @pl.when(lax.axis_index("z") == z)
    def _():
        v = came[...]
        out_before[...] = v
        out_value[...] = v + TOP * conv(v, flat(top[...])) + defect[...]


def next_kernel(z, value, mine, other, defect, ahead, wbuf):
    @pl.when(lax.axis_index("z") == z)
    def _():
        core = lax.axis_index("core")
        wbuf[pl.ds(core * 4, 4)] = mine[...]
        wbuf[pl.ds(4 - core * 4, 4)] = other[...]
        v = value[...]
        ahead[...] = v + TOP * conv(v, flat(wbuf[...])) + defect[...]


def last_kernel(came, before, value, defect, biases, stack, lead, kernels, states, buf, sbuf, sem):
    x, z = lax.axis_index("x"), lax.axis_index("z")
    late = (z == 3) | (z == 5) | (z == 7)
    extra = (x == X - 1) & late

    @pl.when(late)
    def _():
        buf[...] = came[...]

    @pl.when(jnp.logical_not(late))
    def _():
        buf[...] = before[...]

    @pl.when((x == X - 1) & jnp.logical_not(late))
    def _():
        sbuf[3] = value[...]

    @pl.when(extra)
    def _():
        v = buf[...]
        sbuf[3] = v + TOP * conv(v, flat(lead[3])) + defect[...]

    def coarse(q, carry):
        v = buf[...]
        mixed = conv(v, flat(lead[pl.ds(q, 1)]))
        buf[...] = v + COARSE * mixed + stack[pl.ds(q, 1)].reshape(ROWS, CH)
        return carry

    lax.fori_loop(0, x, coarse, 0)

    def fine(i, carry):
        v = buf[...]
        mixed = conv(v, flat(kernels[pl.ds(i, 1)]))

        @pl.when((i == 0) & (x < X - 1))
        def _():
            sbuf[3] = v + COARSE * mixed + stack[pl.ds(x, 1)].reshape(ROWS, CH)

        @pl.when(i == 0)
        def _():
            pltpu.make_async_copy(sbuf.at[3], states.at[3], sem.at[3]).start()

        new = v + FINE * (mixed + biases[pl.ds(i, 1)])
        buf[...] = new
        sbuf[pl.ds(i, 1)] = new.reshape(1, ROWS, CH)
        pltpu.make_async_copy(sbuf.at[i], states.at[i], sem.at[i]).start()
        return carry

    lax.fori_loop(0, 3, fine, 0)
    for i in range(4):
        pltpu.make_async_copy(sbuf.at[i], states.at[i], sem.at[i]).wait()


def call(body, name, outs, convs, args, places, scratch=(), alias=None, out_places=None, limit=16):
    specs = {
        "v": pl.BlockSpec(memory_space=pltpu.VMEM),
        "h": pl.BlockSpec(memory_space=pltpu.HBM),
    }
    out_places = out_places or "v" * len(outs)
    return pl.pallas_call(
        body,
        name=name,
        out_shape=outs,
        in_specs=[specs[p] for p in places],
        out_specs=tuple(specs[p] for p in out_places),
        scratch_shapes=scratch,
        input_output_aliases=alias or {},
        compiler_params=pltpu.CompilerParams(vmem_limit_bytes=limit << 20),
        cost_estimate=pl.CostEstimate(
            flops=convs if convs != 1 else 6 * 10**9,
            bytes_accessed=convs if convs != 1 else 20 * 10**6,
            transcendentals=0,
        ),
    )(*args)


def shards(inputs, guess_states, kernels, biases):
    state = jax.ShapeDtypeStruct((ROWS, CH), jnp.float32)
    weight = jax.ShapeDtypeStruct(WHOLE, jnp.bfloat16)
    buffer = pltpu.VMEM((ROWS, CH), jnp.float32)
    dma = pltpu.SemaphoreType.DMA
    inputs = inputs.reshape(ROWS, CH)
    guess = guess_states.reshape(4, ROWS, CH)
    kernels = kernels.reshape((4,) + WHOLE)
    barrier = lax.optimization_barrier

    def next_layer(v):
        return lax.ppermute(v, LAYER, [(i, (i + 1) % (X * Z)) for i in range(X * Z)])

    def from_ahead(v, r):
        return lax.ppermute(v, "x", [(i, (i - r) % X) for i in range(X)])

    def along_z(v, *pairs):
        return lax.ppermute(v, "z", pairs)

    guess_corner, share = call(
        prepare_kernel, "prepare",
        (state, jax.ShapeDtypeStruct((SHARE, CH), jnp.bfloat16)), 0,
        (guess, inputs, kernels), "hhh", [dma((2,))], limit=63,
    )
    guess_head = next_layer(guess_corner)
    shares = [from_ahead(share, 1), None, from_ahead(share, 3)]
    (kept,) = call(
        load_kernel, "load", (jax.ShapeDtypeStruct((4,) + WHOLE, jnp.bfloat16),), 0,
        (barrier((kernels, guess_corner))[0],), "h", [dma(())],
    )
    shares[1] = from_ahead(barrier((shares[0], kept))[0], 1)
    (point,) = call(
        first_kernel, "first", (state,), 4, (guess_head, kept, biases), "vvv",
    )
    head = next_layer(point)
    first_piece = jnp.stack(barrier((point, *shares))[1:])
    pieces = [first_piece] + [
        lax.ppermute(first_piece, "y", [(i, (i + r) % 4) for i in range(4)]) for r in (1, 3, 2)
    ]
    message, term = call(
        second_kernel, "second", (state, state), 4,
        (head, guess_head, kept, biases),
        "vvvv", [buffer],
    )
    m2, m3, m1 = (from_ahead(message, r) for r in (2, 3, 1))
    pieces, m2, m3 = barrier((pieces, m2, m3))
    pieces += [lax.ppermute(p, "core", [(0, 1), (1, 0)]) for p in pieces]
    term, m3 = barrier((term, m3))
    f3 = lax.ppermute(term, "x", [(0, 3)])
    stacked = jax.ShapeDtypeStruct((X, ROWS, CH), jnp.float32)
    point, stack, lead, top, part = call(
        third_kernel, "third",
        (state, stacked, jax.ShapeDtypeStruct((X,) + WHOLE, jnp.bfloat16), weight,
         jax.ShapeDtypeStruct((4, SHARE, CH), jnp.bfloat16)),
        3, (message, m1, m2, m3, kept, *pieces), "v" * 13,
    )
    hop = along_z(point, *((i, i + 1) for i in range(Z - 1)))
    f3, term, _ = barrier((f3, term, point))
    f2 = lax.ppermute(f3, "x", [(3, 2)])
    f1 = lax.ppermute(term, "x", [(0, 1)])
    next_mine = along_z(part, (3, 2), (5, 4))
    residual, corner, start, stack = call(
        fourth_kernel, "fourth", (state,) * 3 + (stacked,), 1,
        (inputs, hop, point, term, f1, f2, f3, stack, lead), "v" * 9,
    )
    came = along_z(corner, (1, 2))
    (defect,) = call(defect_kernel, "defect", (state,), 1, (corner, start, top), "vvv")
    next_defect = {2: along_z(defect, (3, 2)), 4: along_z(defect, (5, 4))}
    next_mine, _ = barrier((next_mine, defect))
    next_other = lax.ppermute(next_mine, "core", [(0, 1), (1, 0)])
    before, value = start, corner
    for z in (2, 4, 6):
        before, value = call(
            functools.partial(one_kernel, z), f"one{z}", (state, state), 1,
            (came, before, value, top, defect), "vvvvv", alias={1: 0, 2: 1},
        )
        if z < 6:
            (ahead,) = call(
                functools.partial(next_kernel, z), f"next{z}", (state,), 0,
                (value, next_mine, next_other, next_defect[z]), "vvvv",
                [pltpu.VMEM(WHOLE, jnp.bfloat16)],
            )
            came = along_z(ahead, (z, z + 2))
    came = along_z(value, (2, 3), (4, 5), (6, 7))
    (states,) = call(
        last_kernel, "last", (jax.ShapeDtypeStruct((4, ROWS, CH), jnp.float32),), 6,
        (came, before, value, defect, biases, stack, lead, kept), "v" * 8,
        [buffer, pltpu.VMEM((4, ROWS, CH), jnp.float32), dma((4,))], out_places="h",
    )
    volume = (8, 8, 8, CH)
    return states.reshape((4, 1) + volume), residual.reshape((1, 1) + volume)


def solution(mesh):
    finer = Mesh(mesh.devices.reshape(Z, X, 4, 2), LAYER + BATCH)
    return jax.shard_map(
        shards,
        mesh=finer,
        in_specs=(P(BATCH), P(LAYER, BATCH), P(LAYER), P(LAYER)),
        out_specs=(P(LAYER, BATCH), P(LAYER, BATCH)),
        check_vma=False,
    )
```

```python
import functools

import jax
import jax.numpy as jnp
from jax import lax
from jax.experimental import pallas as pl
from jax.experimental.pallas import tpu as pltpu
from jax.sharding import Mesh
from jax.sharding import PartitionSpec as P

X, Z = 4, 8
LAYER, BATCH = ("z", "x"), ("y", "core")
ROWS, CH = 512, 128
TAPS, DEEP = 9, 384
SHARE = TAPS * DEEP // 8
WHOLE = (8, SHARE, CH)
FINE = 2.0 / 128
COARSE = 4 * FINE
TOP = 4 * COARSE


def conv(v, weights):
    t = jnp.tanh(v).reshape(64, 8, CH)
    at = lax.broadcasted_iota(jnp.int32, (64, 8, CH), 1)
    before = jnp.where(at == 0, 0.0, pltpu.roll(t, 1, 1))
    after = jnp.where(at == 7, 0.0, pltpu.roll(t, 7, 1))
    lhs = jnp.concatenate(
        [s.reshape(ROWS, CH).astype(jnp.bfloat16) for s in (before, t, after)], 1
    )
    rhs = jnp.concatenate([weights[n * DEEP : (n + 1) * DEEP] for n in range(TAPS)], 1)
    out = jnp.dot(lhs, rhs, preferred_element_type=jnp.float32)
    edge_y = jnp.zeros((8, 1, 8, CH), jnp.float32)
    edge_x = jnp.zeros((1, 8, 8, CH), jnp.float32)
    total = None
    for dx in range(3):
        for dy in range(3):
            n = dx * 3 + dy
            part = out[:, n * CH : (n + 1) * CH].reshape(8, 8, 8, CH)
            if dy == 0:
                part = jnp.concatenate([edge_y, part[:, :7]], 1)
            if dy == 2:
                part = jnp.concatenate([part[:, 1:], edge_y], 1)
            if dx == 0:
                part = jnp.concatenate([edge_x, part[:7]], 0)
            if dx == 2:
                part = jnp.concatenate([part[1:], edge_x], 0)
            total = part if total is None else total + part
    return total.reshape(ROWS, CH)


def flat(weights):
    return weights.reshape(TAPS * DEEP, CH)


def last_device():
    return (lax.axis_index("x") == X - 1) & (lax.axis_index("z") == Z - 1)


def first_device():
    return (lax.axis_index("x") == 0) & (lax.axis_index("z") == 0)


def prepare_kernel(guess, inputs, kernels, corner, share, sem):
    two = pltpu.make_async_copy(
        kernels.at[0, lax.axis_index("y") * 2 + lax.axis_index("core")], share, sem.at[1]
    )
    two.start()

    @pl.when(last_device())
    def _():
        pltpu.make_async_copy(inputs, corner, sem.at[0]).start()

    @pl.when(jnp.logical_not(last_device()))
    def _():
        pltpu.make_async_copy(guess.at[3], corner, sem.at[0]).start()

    pltpu.make_async_copy(inputs, corner, sem.at[0]).wait()
    two.wait()


def load_kernel(kernels, kept, sem):
    copy = pltpu.make_async_copy(kernels, kept, sem)
    copy.start()
    copy.wait()


def first_kernel(head, kernels, biases, out):
    out[...] = head[...]

    def body(i, carry):
        v = out[...]
        out[...] = v + FINE * (conv(v, flat(kernels[pl.ds(i, 1)])) + biases[pl.ds(i, 1)])
        return carry

    lax.fori_loop(0, 4, body, 0)


def second_kernel(head, guess_head, kernels, biases, message, term, buf):
    @pl.when(first_device())
    def _():
        buf[...] = guess_head[...]

    @pl.when(jnp.logical_not(first_device()))
    def _():
        buf[...] = head[...]

    term[...] = buf[...]

    def body(i, carry):
        v = buf[...]
        mixed = conv(v, flat(kernels[pl.ds(i, 1)]))
        buf[...] = v + FINE * (mixed + biases[pl.ds(i, 1)])

        @pl.when(i == 0)
        def _():
            term[...] += COARSE * mixed

        return carry

    lax.fori_loop(0, 4, body, 0)
    term[...] = buf[...] - term[...]
    x = lax.axis_index("x")

    @pl.when(x == 0)
    def _():
        message[...] = buf[...]

    @pl.when(x > 0)
    def _():
        message[...] = term[...]


def coarse_steps(out, stack, lead, first=0, ready=lambda q: None):
    def body(q, carry):
        ready(q)
        v = out[...]
        mixed = conv(v, flat(lead[pl.ds(q, 1)]))
        out[...] = v + COARSE * mixed + stack[pl.ds(q, 1)].reshape(ROWS, CH)
        return carry

    lax.fori_loop(first, X, body, 0)


def third_kernel(
    m0, m1, m2, m3, kernels, p0, p1, p2, p3, o0, o1, o2, o3, out, stack, lead, top, part
):
    x, y, core = lax.axis_index("x"), lax.axis_index("y"), lax.axis_index("core")
    lead[pl.ds(x, 1)] = kernels[pl.ds(0, 1)]
    for offset, mine, other in ((0, p0, o0), (3, p1, o1), (1, p2, o2), (2, p3, o3)):
        at = lax.rem(y + offset, 4) * 2
        for r in range(1, X):
            q = pl.ds(lax.rem(x + r, X), 1)
            lead[q, pl.ds(at + core, 1)] = mine[r - 1].reshape(1, 1, SHARE, CH)
            lead[q, pl.ds(at + 1 - core, 1)] = other[r - 1].reshape(1, 1, SHARE, CH)
    for r, term in enumerate((m0, m1, m2, m3)):
        stack[pl.ds(lax.rem(x + r, X), 1)] = term[...].reshape(1, ROWS, CH)
    out[...] = stack[0]
    coarse_steps(out, stack, lead, 1)
    top[...] = lead[X - 1]
    part[...] = lead[X - 1, pl.ds(core * 4, 4)]


def begin_kernel(inputs, hop, lead, start, partial):
    z = lax.axis_index("z")

    @pl.when(z == 0)
    def _():
        start[...] = inputs[...]

    @pl.when(z > 0)
    def _():
        start[...] = hop[...]

    v = start[...]
    partial[...] = v + COARSE * conv(v, flat(lead[0]))


def fourth_kernel(partial, point, term, f1, f2, f3, stack, lead, residual, corner, out_stack):
    x = lax.axis_index("x")
    out_stack[1:] = stack[1:]
    for r, first in enumerate((term, f1, f2, f3)):

        @pl.when(x == r)
        def _():
            out_stack[0] = first[...]

    corner[...] = partial[...] + out_stack[0]
    coarse_steps(corner, out_stack, lead, 1)

    @pl.when(x == X - 1)
    def _():
        residual[...] = corner[...] - point[...]

    @pl.when(x != X - 1)
    def _():
        residual[...] = jnp.zeros((ROWS, CH), jnp.float32)


def defect_kernel(corner, start, top, defect):
    v = start[...]
    defect[...] = corner[...] - v - TOP * conv(v, flat(top[...]))


def one_kernel(z, came, before, value, top, defect, out_before, out_value):
    @pl.when(lax.axis_index("z") == z)
    def _():
        v = came[...]
        out_before[...] = v
        out_value[...] = v + TOP * conv(v, flat(top[...])) + defect[...]


def next_kernel(z, value, mine, other, defect, ahead, wbuf):
    @pl.when(lax.axis_index("z") == z)
    def _():
        core = lax.axis_index("core")
        wbuf[pl.ds(core * 4, 4)] = mine[...]
        wbuf[pl.ds(4 - core * 4, 4)] = other[...]
        v = value[...]
        ahead[...] = v + TOP * conv(v, flat(wbuf[...])) + defect[...]


def last_kernel(came, before, value, defect, biases, stack, lead, kernels, states, buf, sbuf, sem):
    x, z = lax.axis_index("x"), lax.axis_index("z")
    late = (z == 3) | (z == 5) | (z == 7)
    extra = (x == X - 1) & late

    @pl.when(late)
    def _():
        buf[...] = came[...]

    @pl.when(jnp.logical_not(late))
    def _():
        buf[...] = before[...]

    @pl.when((x == X - 1) & jnp.logical_not(late))
    def _():
        sbuf[3] = value[...]

    @pl.when(extra)
    def _():
        v = buf[...]
        sbuf[3] = v + TOP * conv(v, flat(lead[3])) + defect[...]

    def coarse(q, carry):
        v = buf[...]
        mixed = conv(v, flat(lead[pl.ds(q, 1)]))
        buf[...] = v + COARSE * mixed + stack[pl.ds(q, 1)].reshape(ROWS, CH)
        return carry

    lax.fori_loop(0, x, coarse, 0)

    def fine(i, carry):
        v = buf[...]
        mixed = conv(v, flat(kernels[pl.ds(i, 1)]))

        @pl.when((i == 0) & (x < X - 1))
        def _():
            sbuf[3] = v + COARSE * mixed + stack[pl.ds(x, 1)].reshape(ROWS, CH)

        @pl.when(i == 0)
        def _():
            pltpu.make_async_copy(sbuf.at[3], states.at[3], sem.at[3]).start()

        new = v + FINE * (mixed + biases[pl.ds(i, 1)])
        buf[...] = new
        sbuf[pl.ds(i, 1)] = new.reshape(1, ROWS, CH)
        pltpu.make_async_copy(sbuf.at[i], states.at[i], sem.at[i]).start()
        return carry

    lax.fori_loop(0, 3, fine, 0)
    for i in range(4):
        pltpu.make_async_copy(sbuf.at[i], states.at[i], sem.at[i]).wait()


def call(body, name, outs, convs, args, places, scratch=(), alias=None, out_places=None, limit=16):
    specs = {
        "v": pl.BlockSpec(memory_space=pltpu.VMEM),
        "h": pl.BlockSpec(memory_space=pltpu.HBM),
    }
    out_places = out_places or "v" * len(outs)
    return pl.pallas_call(
        body,
        name=name,
        out_shape=outs,
        in_specs=[specs[p] for p in places],
        out_specs=tuple(specs[p] for p in out_places),
        scratch_shapes=scratch,
        input_output_aliases=alias or {},
        compiler_params=pltpu.CompilerParams(vmem_limit_bytes=limit << 20),
        cost_estimate=pl.CostEstimate(
            flops=(0, 6, 30)[convs] * 10**9 if convs < 3 else 0,
            bytes_accessed=(0, 20, 100)[convs] * 10**6 if convs < 3 else 0,
            transcendentals=0,
        ),
    )(*args)


def shards(inputs, guess_states, kernels, biases):
    state = jax.ShapeDtypeStruct((ROWS, CH), jnp.float32)
    weight = jax.ShapeDtypeStruct(WHOLE, jnp.bfloat16)
    buffer = pltpu.VMEM((ROWS, CH), jnp.float32)
    dma = pltpu.SemaphoreType.DMA
    inputs = inputs.reshape(ROWS, CH)
    guess = guess_states.reshape(4, ROWS, CH)
    kernels = kernels.reshape((4,) + WHOLE)
    barrier = lax.optimization_barrier

    def next_layer(v):
        return lax.ppermute(v, LAYER, [(i, (i + 1) % (X * Z)) for i in range(X * Z)])

    def from_ahead(v, r):
        return lax.ppermute(v, "x", [(i, (i - r) % X) for i in range(X)])

    def along_z(v, *pairs):
        return lax.ppermute(v, "z", pairs)

    guess_corner, share = call(
        prepare_kernel, "prepare",
        (state, jax.ShapeDtypeStruct((SHARE, CH), jnp.bfloat16)), 0,
        (guess, inputs, kernels), "hhh", [dma((2,))], limit=63,
    )
    guess_head = next_layer(guess_corner)
    shares = [from_ahead(share, 1), None, from_ahead(share, 3)]
    (kept,) = call(
        load_kernel, "load", (jax.ShapeDtypeStruct((4,) + WHOLE, jnp.bfloat16),), 0,
        (barrier((kernels, guess_corner))[0],), "h", [dma(())],
    )
    shares[1] = from_ahead(barrier((shares[0], kept))[0], 1)
    guess_head, *shares = barrier((guess_head, *shares))
    (point,) = call(
        first_kernel, "first", (state,), 4, (guess_head, kept, biases), "vvv",
    )
    head = next_layer(point)
    first_piece = jnp.stack(barrier((point, *shares))[1:])
    pieces = [first_piece] + [
        lax.ppermute(first_piece, "y", [(i, (i + r) % 4) for i in range(4)]) for r in (1, 3, 2)
    ]
    message, term = call(
        second_kernel, "second", (state, state), 1,
        (head, guess_head, kept, biases),
        "vvvv", [buffer],
    )
    m2, m3, m1 = (from_ahead(message, r) for r in (2, 3, 1))
    pieces, m2, m3 = barrier((pieces, m2, m3))
    pieces[3], m1 = barrier((pieces[3], m1))
    pieces += [lax.ppermute(p, "core", [(0, 1), (1, 0)]) for p in pieces]
    term, m3 = barrier((term, m3))
    f3 = lax.ppermute(term, "x", [(0, 3)])
    stacked = jax.ShapeDtypeStruct((X, ROWS, CH), jnp.float32)
    point, stack, lead, top, part = call(
        third_kernel, "third",
        (state, stacked, jax.ShapeDtypeStruct((X,) + WHOLE, jnp.bfloat16), weight,
         jax.ShapeDtypeStruct((4, SHARE, CH), jnp.bfloat16)),
        3, (message, m1, m2, m3, kept, *pieces), "v" * 13,
    )
    hop = along_z(point, *((i, i + 1) for i in range(Z - 1)))
    f3, term, _ = barrier((f3, term, point))
    f2 = lax.ppermute(f3, "x", [(3, 2)])
    f1 = lax.ppermute(term, "x", [(0, 1)])
    next_mine = along_z(part, (3, 2), (5, 4))
    start, partial = call(
        begin_kernel, "begin", (state, state), 2, (inputs, hop, lead), "vvv",
    )
    residual, corner, stack = call(
        fourth_kernel, "fourth", (state, state, stacked), 1,
        (partial, point, term, f1, f2, f3, stack, lead), "v" * 8,
    )
    came = along_z(corner, (1, 2))
    (defect,) = call(defect_kernel, "defect", (state,), 1, (corner, start, top), "vvv")
    next_defect = {2: along_z(defect, (3, 2)), 4: along_z(defect, (5, 4))}
    next_mine, _ = barrier((next_mine, defect))
    next_other = lax.ppermute(next_mine, "core", [(0, 1), (1, 0)])
    before, value = start, corner
    for z in (2, 4, 6):
        before, value = call(
            functools.partial(one_kernel, z), f"one{z}", (state, state), 1,
            (came, before, value, top, defect), "vvvvv", alias={1: 0, 2: 1},
        )
        if z < 6:
            (ahead,) = call(
                functools.partial(next_kernel, z), f"next{z}", (state,), 0,
                (value, next_mine, next_other, next_defect[z]), "vvvv",
                [pltpu.VMEM(WHOLE, jnp.bfloat16)],
            )
            came = along_z(ahead, (z, z + 2))
    came = along_z(value, (2, 3), (4, 5), (6, 7))
    (states,) = call(
        last_kernel, "last", (jax.ShapeDtypeStruct((4, ROWS, CH), jnp.float32),), 6,
        (came, before, value, defect, biases, stack, lead, kept), "v" * 8,
        [buffer, pltpu.VMEM((4, ROWS, CH), jnp.float32), dma((4,))], out_places="h",
    )
    volume = (8, 8, 8, CH)
    return states.reshape((4, 1) + volume), residual.reshape((1, 1) + volume)


def solution(mesh):
    finer = Mesh(mesh.devices.reshape(Z, X, 4, 2), LAYER + BATCH)
    return jax.shard_map(
        shards,
        mesh=finer,
        in_specs=(P(BATCH), P(LAYER, BATCH), P(LAYER), P(LAYER)),
        out_specs=(P(LAYER, BATCH), P(LAYER, BATCH)),
        check_vma=False,
    )
```

```python
import functools

import jax
import jax.numpy as jnp
from jax import lax
from jax.experimental import pallas as pl
from jax.experimental.pallas import tpu as pltpu
from jax.sharding import Mesh
from jax.sharding import PartitionSpec as P

X, Z = 4, 8
LAYER, BATCH = ("z", "x"), ("y", "core")
ROWS, CH = 512, 128
TAPS, DEEP = 9, 384
SHARE = TAPS * DEEP // 8
WHOLE = (8, SHARE, CH)
FINE = 2.0 / 128
COARSE = 4 * FINE
TOP = 4 * COARSE


def conv(v, weights):
    t = jnp.tanh(v).reshape(64, 8, CH)
    at = lax.broadcasted_iota(jnp.int32, (64, 8, CH), 1)
    before = jnp.where(at == 0, 0.0, pltpu.roll(t, 1, 1))
    after = jnp.where(at == 7, 0.0, pltpu.roll(t, 7, 1))
    lhs = jnp.concatenate(
        [s.reshape(ROWS, CH).astype(jnp.bfloat16) for s in (before, t, after)], 1
    )
    rhs = jnp.concatenate([weights[n * DEEP : (n + 1) * DEEP] for n in range(TAPS)], 1)
    out = jnp.dot(lhs, rhs, preferred_element_type=jnp.float32)
    edge_y = jnp.zeros((8, 1, 8, CH), jnp.float32)
    edge_x = jnp.zeros((1, 8, 8, CH), jnp.float32)
    total = None
    for dx in range(3):
        for dy in range(3):
            n = dx * 3 + dy
            part = out[:, n * CH : (n + 1) * CH].reshape(8, 8, 8, CH)
            if dy == 0:
                part = jnp.concatenate([edge_y, part[:, :7]], 1)
            if dy == 2:
                part = jnp.concatenate([part[:, 1:], edge_y], 1)
            if dx == 0:
                part = jnp.concatenate([edge_x, part[:7]], 0)
            if dx == 2:
                part = jnp.concatenate([part[1:], edge_x], 0)
            total = part if total is None else total + part
    return total.reshape(ROWS, CH)


def flat(weights):
    return weights.reshape(TAPS * DEEP, CH)


def last_device():
    return (lax.axis_index("x") == X - 1) & (lax.axis_index("z") == Z - 1)


def first_device():
    return (lax.axis_index("x") == 0) & (lax.axis_index("z") == 0)


def prepare_kernel(guess, inputs, kernels, corner, share, sem):
    two = pltpu.make_async_copy(
        kernels.at[0, lax.axis_index("y") * 2 + lax.axis_index("core")], share, sem.at[1]
    )
    two.start()

    @pl.when(last_device())
    def _():
        pltpu.make_async_copy(inputs, corner, sem.at[0]).start()

    @pl.when(jnp.logical_not(last_device()))
    def _():
        pltpu.make_async_copy(guess.at[3], corner, sem.at[0]).start()

    pltpu.make_async_copy(inputs, corner, sem.at[0]).wait()
    two.wait()


def load_kernel(kernels, kept, sem):
    copy = pltpu.make_async_copy(kernels, kept, sem)
    copy.start()
    copy.wait()


def first_kernel(head, kernels, biases, out):
    out[...] = head[...]

    def body(i, carry):
        v = out[...]
        out[...] = v + FINE * (conv(v, flat(kernels[pl.ds(i, 1)])) + biases[pl.ds(i, 1)])
        return carry

    lax.fori_loop(0, 4, body, 0)


def second_kernel(head, guess_head, kernels, biases, message, term, buf):
    @pl.when(first_device())
    def _():
        buf[...] = guess_head[...]

    @pl.when(jnp.logical_not(first_device()))
    def _():
        buf[...] = head[...]

    term[...] = buf[...]

    def body(i, carry):
        v = buf[...]
        mixed = conv(v, flat(kernels[pl.ds(i, 1)]))
        buf[...] = v + FINE * (mixed + biases[pl.ds(i, 1)])

        @pl.when(i == 0)
        def _():
            term[...] += COARSE * mixed

        return carry

    lax.fori_loop(0, 4, body, 0)
    term[...] = buf[...] - term[...]
    x = lax.axis_index("x")

    @pl.when(x == 0)
    def _():
        message[...] = buf[...]

    @pl.when(x > 0)
    def _():
        message[...] = term[...]


def coarse_steps(out, stack, lead, first=0, ready=lambda q: None):
    def body(q, carry):
        ready(q)
        v = out[...]
        mixed = conv(v, flat(lead[pl.ds(q, 1)]))
        out[...] = v + COARSE * mixed + stack[pl.ds(q, 1)].reshape(ROWS, CH)
        return carry

    lax.fori_loop(first, X, body, 0)


def third_kernel(
    m0, m1, m2, m3, kernels, p0, p1, p2, p3, o0, o1, o2, o3, out, stack, lead, top, part
):
    x, y, core = lax.axis_index("x"), lax.axis_index("y"), lax.axis_index("core")
    lead[pl.ds(x, 1)] = kernels[pl.ds(0, 1)]
    for offset, mine, other in ((0, p0, o0), (3, p1, o1), (1, p2, o2), (2, p3, o3)):
        at = lax.rem(y + offset, 4) * 2
        for r in range(1, X):
            q = pl.ds(lax.rem(x + r, X), 1)
            lead[q, pl.ds(at + core, 1)] = mine[r - 1].reshape(1, 1, SHARE, CH)
            lead[q, pl.ds(at + 1 - core, 1)] = other[r - 1].reshape(1, 1, SHARE, CH)
    for r, term in enumerate((m0, m1, m2, m3)):
        stack[pl.ds(lax.rem(x + r, X), 1)] = term[...].reshape(1, ROWS, CH)
    out[...] = stack[0]
    coarse_steps(out, stack, lead, 1)
    top[...] = lead[X - 1]
    part[...] = lead[X - 1, pl.ds(core * 4, 4)]


def begin_kernel(inputs, hop, lead, start, partial):
    z = lax.axis_index("z")

    @pl.when(z == 0)
    def _():
        start[...] = inputs[...]

    @pl.when(z > 0)
    def _():
        start[...] = hop[...]

    v = start[...]
    partial[...] = v + COARSE * conv(v, flat(lead[0]))


def fourth_kernel(partial, point, term, f1, f2, f3, stack, lead, residual, corner, out_stack):
    x = lax.axis_index("x")
    out_stack[1:] = stack[1:]
    for r, first in enumerate((term, f1, f2, f3)):

        @pl.when(x == r)
        def _():
            out_stack[0] = first[...]

    corner[...] = partial[...] + out_stack[0]
    coarse_steps(corner, out_stack, lead, 1)

    @pl.when(x == X - 1)
    def _():
        residual[...] = corner[...] - point[...]

    @pl.when(x != X - 1)
    def _():
        residual[...] = jnp.zeros((ROWS, CH), jnp.float32)


def defect_kernel(corner, start, top, defect):
    v = start[...]
    defect[...] = corner[...] - v - TOP * conv(v, flat(top[...]))


def one_kernel(z, came, before, value, top, defect, out_before, out_value):
    @pl.when(lax.axis_index("z") == z)
    def _():
        v = came[...]
        out_before[...] = v
        out_value[...] = v + TOP * conv(v, flat(top[...])) + defect[...]


def next_kernel(z, value, mine, other, defect, ahead, wbuf):
    @pl.when(lax.axis_index("z") == z)
    def _():
        core = lax.axis_index("core")
        wbuf[pl.ds(core * 4, 4)] = mine[...]
        wbuf[pl.ds(4 - core * 4, 4)] = other[...]
        v = value[...]
        ahead[...] = v + TOP * conv(v, flat(wbuf[...])) + defect[...]


def last_kernel(came, before, value, defect, biases, stack, lead, kernels, states, buf, sbuf, sem):
    x, z = lax.axis_index("x"), lax.axis_index("z")
    late = (z == 3) | (z == 5) | (z == 7)
    extra = (x == X - 1) & late

    @pl.when(late)
    def _():
        buf[...] = came[...]

    @pl.when(jnp.logical_not(late))
    def _():
        buf[...] = before[...]

    @pl.when((x == X - 1) & jnp.logical_not(late))
    def _():
        sbuf[3] = value[...]

    @pl.when(extra)
    def _():
        v = buf[...]
        sbuf[3] = v + TOP * conv(v, flat(lead[3])) + defect[...]

    def coarse(q, carry):
        v = buf[...]
        mixed = conv(v, flat(lead[pl.ds(q, 1)]))
        buf[...] = v + COARSE * mixed + stack[pl.ds(q, 1)].reshape(ROWS, CH)
        return carry

    lax.fori_loop(0, x, coarse, 0)

    def fine(i, carry):
        v = buf[...]
        mixed = conv(v, flat(kernels[pl.ds(i, 1)]))

        @pl.when((i == 0) & (x < X - 1))
        def _():
            sbuf[3] = v + COARSE * mixed + stack[pl.ds(x, 1)].reshape(ROWS, CH)

        @pl.when(i == 0)
        def _():
            pltpu.make_async_copy(sbuf.at[3], states.at[3], sem.at[3]).start()

        new = v + FINE * (mixed + biases[pl.ds(i, 1)])
        buf[...] = new
        sbuf[pl.ds(i, 1)] = new.reshape(1, ROWS, CH)
        pltpu.make_async_copy(sbuf.at[i], states.at[i], sem.at[i]).start()
        return carry

    lax.fori_loop(0, 3, fine, 0)
    for i in range(4):
        pltpu.make_async_copy(sbuf.at[i], states.at[i], sem.at[i]).wait()


def call(body, name, outs, convs, args, places, scratch=(), alias=None, out_places=None, limit=16):
    specs = {
        "v": pl.BlockSpec(memory_space=pltpu.VMEM),
        "h": pl.BlockSpec(memory_space=pltpu.HBM),
    }
    out_places = out_places or "v" * len(outs)
    return pl.pallas_call(
        body,
        name=name,
        out_shape=outs,
        in_specs=[specs[p] for p in places],
        out_specs=tuple(specs[p] for p in out_places),
        scratch_shapes=scratch,
        input_output_aliases=alias or {},
        compiler_params=pltpu.CompilerParams(vmem_limit_bytes=limit << 20),
        cost_estimate=pl.CostEstimate(
            flops=(0, 6, 30)[convs] * 10**9 if convs < 3 else 0,
            bytes_accessed=(0, 20, 100)[convs] * 10**6 if convs < 3 else 0,
            transcendentals=0,
        ),
    )(*args)


def shards(inputs, guess_states, kernels, biases):
    state = jax.ShapeDtypeStruct((ROWS, CH), jnp.float32)
    weight = jax.ShapeDtypeStruct(WHOLE, jnp.bfloat16)
    buffer = pltpu.VMEM((ROWS, CH), jnp.float32)
    dma = pltpu.SemaphoreType.DMA
    inputs = inputs.reshape(ROWS, CH)
    guess = guess_states.reshape(4, ROWS, CH)
    kernels = kernels.reshape((4,) + WHOLE)
    barrier = lax.optimization_barrier

    def next_layer(v):
        return lax.ppermute(v, LAYER, [(i, (i + 1) % (X * Z)) for i in range(X * Z)])

    def from_ahead(v, r):
        return lax.ppermute(v, "x", [(i, (i - r) % X) for i in range(X)])

    def along_z(v, *pairs):
        return lax.ppermute(v, "z", pairs)

    guess_corner, share = call(
        prepare_kernel, "prepare",
        (state, jax.ShapeDtypeStruct((SHARE, CH), jnp.bfloat16)), 0,
        (guess, inputs, kernels), "hhh", [dma((2,))], limit=63,
    )
    guess_head = next_layer(guess_corner)
    shares = [from_ahead(share, 1), None, from_ahead(share, 3)]
    (kept,) = call(
        load_kernel, "load", (jax.ShapeDtypeStruct((4,) + WHOLE, jnp.bfloat16),), 0,
        (barrier((kernels, guess_corner))[0],), "h", [dma(())],
    )
    shares[1] = from_ahead(barrier((shares[0], kept))[0], 1)
    guess_head, shares[2] = barrier((guess_head, shares[2]))
    (point,) = call(
        first_kernel, "first", (state,), 4, (guess_head, kept, biases), "vvv",
    )
    head = next_layer(point)
    first_piece = jnp.stack(barrier((point, *shares))[1:])
    pieces = [first_piece] + [
        lax.ppermute(first_piece, "y", [(i, (i + r) % 4) for i in range(4)]) for r in (1, 3)
    ]
    message, term = call(
        second_kernel, "second", (state, state), 1,
        (head, guess_head, kept, biases),
        "vvvv", [buffer],
    )
    m2, m3, m1 = (from_ahead(message, r) for r in (2, 3, 1))
    pieces[1], message = barrier((pieces[1], message))
    pieces.append(lax.ppermute(pieces[1], "y", [(i, (i + 1) % 4) for i in range(4)]))
    pieces, m1, m2, m3 = barrier((pieces, m1, m2, m3))
    pieces += [lax.ppermute(p, "core", [(0, 1), (1, 0)]) for p in pieces]
    term, m3 = barrier((term, m3))
    f3 = lax.ppermute(term, "x", [(0, 3)])
    f1 = lax.ppermute(term, "x", [(0, 1)])
    stacked = jax.ShapeDtypeStruct((X, ROWS, CH), jnp.float32)
    point, stack, lead, top, part = call(
        third_kernel, "third",
        (state, stacked, jax.ShapeDtypeStruct((X,) + WHOLE, jnp.bfloat16), weight,
         jax.ShapeDtypeStruct((4, SHARE, CH), jnp.bfloat16)),
        3, (message, m1, m2, m3, kept, *pieces), "v" * 13,
    )
    hop = along_z(point, *((i, i + 1) for i in range(Z - 1)))
    f1, _ = barrier((f1, point))
    f2 = lax.ppermute(f1, "x", [(1, 2)])
    next_mine = along_z(part, (3, 2), (5, 4))
    start, partial = call(
        begin_kernel, "begin", (state, state), 2, (inputs, hop, lead), "vvv",
    )
    residual, corner, stack = call(
        fourth_kernel, "fourth", (state, state, stacked), 1,
        (partial, point, term, f1, f2, f3, stack, lead), "v" * 8,
    )
    came = along_z(corner, (1, 2))
    (defect,) = call(defect_kernel, "defect", (state,), 1, (corner, start, top), "vvv")
    next_defect = {2: along_z(defect, (3, 2)), 4: along_z(defect, (5, 4))}
    next_mine, _ = barrier((next_mine, defect))
    next_other = lax.ppermute(next_mine, "core", [(0, 1), (1, 0)])
    before, value = start, corner
    for z in (2, 4, 6):
        before, value = call(
            functools.partial(one_kernel, z), f"one{z}", (state, state), 1,
            (came, before, value, top, defect), "vvvvv", alias={1: 0, 2: 1},
        )
        if z < 6:
            (ahead,) = call(
                functools.partial(next_kernel, z), f"next{z}", (state,), 0,
                (value, next_mine, next_other, next_defect[z]), "vvvv",
                [pltpu.VMEM(WHOLE, jnp.bfloat16)],
            )
            came = along_z(ahead, (z, z + 2))
    came = along_z(value, (2, 3), (4, 5), (6, 7))
    (states,) = call(
        last_kernel, "last", (jax.ShapeDtypeStruct((4, ROWS, CH), jnp.float32),), 6,
        (came, before, value, defect, biases, stack, lead, kept), "v" * 8,
        [buffer, pltpu.VMEM((4, ROWS, CH), jnp.float32), dma((4,))], out_places="h",
    )
    volume = (8, 8, 8, CH)
    return states.reshape((4, 1) + volume), residual.reshape((1, 1) + volume)


def solution(mesh):
    finer = Mesh(mesh.devices.reshape(Z, X, 4, 2), LAYER + BATCH)
    return jax.shard_map(
        shards,
        mesh=finer,
        in_specs=(P(BATCH), P(LAYER, BATCH), P(LAYER), P(LAYER)),
        out_specs=(P(LAYER, BATCH), P(LAYER, BATCH)),
        check_vma=False,
    )
```

```python
import functools

import jax
import jax.numpy as jnp
from jax import lax
from jax.experimental import pallas as pl
from jax.experimental.pallas import tpu as pltpu
from jax.sharding import Mesh
from jax.sharding import PartitionSpec as P

X, Z = 4, 8
LAYER, BATCH = ("z", "x"), ("y", "core")
ROWS, CH = 512, 128
TAPS, DEEP = 9, 384
SHARE = TAPS * DEEP // 8
WHOLE = (8, SHARE, CH)
FINE = 2.0 / 128
COARSE = 4 * FINE
TOP = 4 * COARSE


def conv(v, weights):
    t = jnp.tanh(v).reshape(64, 8, CH)
    at = lax.broadcasted_iota(jnp.int32, (64, 8, CH), 1)
    before = jnp.where(at == 0, 0.0, pltpu.roll(t, 1, 1))
    after = jnp.where(at == 7, 0.0, pltpu.roll(t, 7, 1))
    lhs = jnp.concatenate(
        [s.reshape(ROWS, CH).astype(jnp.bfloat16) for s in (before, t, after)], 1
    )
    rhs = jnp.concatenate([weights[n * DEEP : (n + 1) * DEEP] for n in range(TAPS)], 1)
    out = jnp.dot(lhs, rhs, preferred_element_type=jnp.float32)
    edge_y = jnp.zeros((8, 1, 8, CH), jnp.float32)
    edge_x = jnp.zeros((1, 8, 8, CH), jnp.float32)
    total = None
    for dx in range(3):
        for dy in range(3):
            n = dx * 3 + dy
            part = out[:, n * CH : (n + 1) * CH].reshape(8, 8, 8, CH)
            if dy == 0:
                part = jnp.concatenate([edge_y, part[:, :7]], 1)
            if dy == 2:
                part = jnp.concatenate([part[:, 1:], edge_y], 1)
            if dx == 0:
                part = jnp.concatenate([edge_x, part[:7]], 0)
            if dx == 2:
                part = jnp.concatenate([part[1:], edge_x], 0)
            total = part if total is None else total + part
    return total.reshape(ROWS, CH)


def flat(weights):
    return weights.reshape(TAPS * DEEP, CH)


def last_device():
    return (lax.axis_index("x") == X - 1) & (lax.axis_index("z") == Z - 1)


def first_device():
    return (lax.axis_index("x") == 0) & (lax.axis_index("z") == 0)


def prepare_kernel(guess, inputs, kernels, corner, share, sem):
    two = pltpu.make_async_copy(
        kernels.at[0, lax.axis_index("y") * 2 + lax.axis_index("core")], share, sem.at[1]
    )
    two.start()

    @pl.when(last_device())
    def _():
        pltpu.make_async_copy(inputs, corner, sem.at[0]).start()

    @pl.when(jnp.logical_not(last_device()))
    def _():
        pltpu.make_async_copy(guess.at[3], corner, sem.at[0]).start()

    pltpu.make_async_copy(inputs, corner, sem.at[0]).wait()
    two.wait()


def load_kernel(kernels, kept, sem):
    copy = pltpu.make_async_copy(kernels, kept, sem)
    copy.start()
    copy.wait()


def first_kernel(head, kernels, biases, out):
    out[...] = head[...]

    def body(i, carry):
        v = out[...]
        out[...] = v + FINE * (conv(v, flat(kernels[pl.ds(i, 1)])) + biases[pl.ds(i, 1)])
        return carry

    lax.fori_loop(0, 4, body, 0)


def second_kernel(head, guess_head, kernels, biases, message, term, buf):
    @pl.when(first_device())
    def _():
        buf[...] = guess_head[...]

    @pl.when(jnp.logical_not(first_device()))
    def _():
        buf[...] = head[...]

    term[...] = buf[...]

    def body(i, carry):
        v = buf[...]
        mixed = conv(v, flat(kernels[pl.ds(i, 1)]))
        buf[...] = v + FINE * (mixed + biases[pl.ds(i, 1)])

        @pl.when(i == 0)
        def _():
            term[...] += COARSE * mixed

        return carry

    lax.fori_loop(0, 4, body, 0)
    term[...] = buf[...] - term[...]
    x = lax.axis_index("x")

    @pl.when(x == 0)
    def _():
        message[...] = buf[...]

    @pl.when(x > 0)
    def _():
        message[...] = term[...]


def coarse_steps(out, stack, lead, first=0, ready=lambda q: None):
    def body(q, carry):
        ready(q)
        v = out[...]
        mixed = conv(v, flat(lead[pl.ds(q, 1)]))
        out[...] = v + COARSE * mixed + stack[pl.ds(q, 1)].reshape(ROWS, CH)
        return carry

    lax.fori_loop(first, X, body, 0)


def third_kernel(
    m0, m1, m2, m3, kernels, p0, p1, p2, p3, o0, o1, o2, o3, out, stack, lead, top, part
):
    x, y, core = lax.axis_index("x"), lax.axis_index("y"), lax.axis_index("core")
    lead[pl.ds(x, 1)] = kernels[pl.ds(0, 1)]
    for offset, mine, other in ((0, p0, o0), (3, p1, o1), (1, p2, o2), (2, p3, o3)):
        at = lax.rem(y + offset, 4) * 2
        for r in range(1, X):
            q = pl.ds(lax.rem(x + r, X), 1)
            lead[q, pl.ds(at + core, 1)] = mine[r - 1].reshape(1, 1, SHARE, CH)
            lead[q, pl.ds(at + 1 - core, 1)] = other[r - 1].reshape(1, 1, SHARE, CH)
    for r, term in enumerate((m0, m1, m2, m3)):
        stack[pl.ds(lax.rem(x + r, X), 1)] = term[...].reshape(1, ROWS, CH)
    out[...] = stack[0]
    coarse_steps(out, stack, lead, 1)
    top[...] = lead[X - 1]
    part[...] = lead[X - 1, pl.ds(core * 4, 4)]


def fourth_kernel(
    inputs, hop, point, term, f1, f2, f3, stack, lead, residual, corner, start, out_stack
):
    x, z = lax.axis_index("x"), lax.axis_index("z")
    out_stack[1:] = stack[1:]
    for r, first in enumerate((term, f1, f2, f3)):

        @pl.when(x == r)
        def _():
            out_stack[0] = first[...]


    @pl.when(z == 0)
    def _():
        start[...] = inputs[...]

    @pl.when(z > 0)
    def _():
        start[...] = hop[...]

    corner[...] = start[...]
    coarse_steps(corner, out_stack, lead)

    @pl.when(x == X - 1)
    def _():
        residual[...] = corner[...] - point[...]

    @pl.when(x != X - 1)
    def _():
        residual[...] = jnp.zeros((ROWS, CH), jnp.float32)


def defect_kernel(corner, start, top, defect):
    v = start[...]
    defect[...] = corner[...] - v - TOP * conv(v, flat(top[...]))


def one_kernel(z, came, before, value, top, defect, out_before, out_value):
    @pl.when(lax.axis_index("z") == z)
    def _():
        v = came[...]
        out_before[...] = v
        out_value[...] = v + TOP * conv(v, flat(top[...])) + defect[...]


def next_kernel(z, value, mine, other, defect, ahead, wbuf):
    @pl.when(lax.axis_index("z") == z)
    def _():
        core = lax.axis_index("core")
        wbuf[pl.ds(core * 4, 4)] = mine[...]
        wbuf[pl.ds(4 - core * 4, 4)] = other[...]
        v = value[...]
        ahead[...] = v + TOP * conv(v, flat(wbuf[...])) + defect[...]


def last_kernel(came, before, value, defect, biases, stack, lead, kernels, states, buf, sbuf, sem):
    x, z = lax.axis_index("x"), lax.axis_index("z")
    late = (z == 3) | (z == 5) | (z == 7)
    extra = (x == X - 1) & late

    @pl.when(late)
    def _():
        buf[...] = came[...]

    @pl.when(jnp.logical_not(late))
    def _():
        buf[...] = before[...]

    @pl.when((x == X - 1) & jnp.logical_not(late))
    def _():
        sbuf[3] = value[...]

    @pl.when(extra)
    def _():
        v = buf[...]
        sbuf[3] = v + TOP * conv(v, flat(lead[3])) + defect[...]

    def coarse(q, carry):
        v = buf[...]
        mixed = conv(v, flat(lead[pl.ds(q, 1)]))
        buf[...] = v + COARSE * mixed + stack[pl.ds(q, 1)].reshape(ROWS, CH)
        return carry

    lax.fori_loop(0, x, coarse, 0)

    def fine(i, carry):
        v = buf[...]
        mixed = conv(v, flat(kernels[pl.ds(i, 1)]))

        @pl.when((i == 0) & (x < X - 1))
        def _():
            sbuf[3] = v + COARSE * mixed + stack[pl.ds(x, 1)].reshape(ROWS, CH)

        @pl.when(i == 0)
        def _():
            pltpu.make_async_copy(sbuf.at[3], states.at[3], sem.at[3]).start()

        new = v + FINE * (mixed + biases[pl.ds(i, 1)])
        buf[...] = new
        sbuf[pl.ds(i, 1)] = new.reshape(1, ROWS, CH)
        pltpu.make_async_copy(sbuf.at[i], states.at[i], sem.at[i]).start()
        return carry

    lax.fori_loop(0, 3, fine, 0)
    for i in range(4):
        pltpu.make_async_copy(sbuf.at[i], states.at[i], sem.at[i]).wait()


def call(body, name, outs, convs, args, places, scratch=(), alias=None, out_places=None, limit=16):
    specs = {
        "v": pl.BlockSpec(memory_space=pltpu.VMEM),
        "h": pl.BlockSpec(memory_space=pltpu.HBM),
    }
    out_places = out_places or "v" * len(outs)
    return pl.pallas_call(
        body,
        name=name,
        out_shape=outs,
        in_specs=[specs[p] for p in places],
        out_specs=tuple(specs[p] for p in out_places),
        scratch_shapes=scratch,
        input_output_aliases=alias or {},
        compiler_params=pltpu.CompilerParams(vmem_limit_bytes=limit << 20),
        cost_estimate=pl.CostEstimate(
            flops=convs if convs != 1 else 6 * 10**9,
            bytes_accessed=convs if convs != 1 else 20 * 10**6,
            transcendentals=0,
        ),
    )(*args)


def shards(inputs, guess_states, kernels, biases):
    state = jax.ShapeDtypeStruct((ROWS, CH), jnp.float32)
    weight = jax.ShapeDtypeStruct(WHOLE, jnp.bfloat16)
    buffer = pltpu.VMEM((ROWS, CH), jnp.float32)
    dma = pltpu.SemaphoreType.DMA
    inputs = inputs.reshape(ROWS, CH)
    guess = guess_states.reshape(4, ROWS, CH)
    kernels = kernels.reshape((4,) + WHOLE)
    barrier = lax.optimization_barrier

    def next_layer(v):
        return lax.ppermute(v, LAYER, [(i, (i + 1) % (X * Z)) for i in range(X * Z)])

    def from_ahead(v, r):
        return lax.ppermute(v, "x", [(i, (i - r) % X) for i in range(X)])

    def along_z(v, *pairs):
        return lax.ppermute(v, "z", pairs)

    guess_corner, share = call(
        prepare_kernel, "prepare",
        (state, jax.ShapeDtypeStruct((SHARE, CH), jnp.bfloat16)), 0,
        (guess, inputs, kernels), "hhh", [dma((2,))], limit=63,
    )
    guess_head = next_layer(guess_corner)
    shares = [from_ahead(share, 1), None, from_ahead(share, 3)]
    (kept,) = call(
        load_kernel, "load", (jax.ShapeDtypeStruct((4,) + WHOLE, jnp.bfloat16),), 0,
        (barrier((kernels, guess_corner))[0],), "h", [dma(())],
    )
    shares[1] = from_ahead(barrier((shares[0], kept))[0], 1)
    (point,) = call(
        first_kernel, "first", (state,), 4, (guess_head, kept, biases), "vvv",
    )
    head = next_layer(point)
    first_piece = jnp.stack(barrier((point, *shares))[1:])
    pieces = [first_piece] + [
        lax.ppermute(first_piece, "y", [(i, (i + r) % 4) for i in range(4)]) for r in (1, 3, 2)
    ]
    message, term = call(
        second_kernel, "second", (state, state), 4,
        (head, guess_head, kept, biases),
        "vvvv", [buffer],
    )
    m2, m3, m1 = (from_ahead(message, r) for r in (2, 3, 1))
    pieces, m2, m3 = barrier((pieces, m2, m3))
    pieces += [lax.ppermute(p, "core", [(0, 1), (1, 0)]) for p in pieces]
    term, m3 = barrier((term, m3))
    f1, f3 = (lax.ppermute(term, "x", [(0, r)]) for r in (1, 3))
    stacked = jax.ShapeDtypeStruct((X, ROWS, CH), jnp.float32)
    point, stack, lead, top, part = call(
        third_kernel, "third",
        (state, stacked, jax.ShapeDtypeStruct((X,) + WHOLE, jnp.bfloat16), weight,
         jax.ShapeDtypeStruct((4, SHARE, CH), jnp.bfloat16)),
        3, (message, m1, m2, m3, kept, *pieces), "v" * 13,
    )
    hop = along_z(point, *((i, i + 1) for i in range(Z - 1)))
    f1, hop_point = barrier((f1, point))
    f2 = lax.ppermute(f1, "x", [(1, 2)])
    next_mine = along_z(part, (3, 2), (5, 4))
    residual, corner, start, stack = call(
        fourth_kernel, "fourth", (state,) * 3 + (stacked,), 1,
        (inputs, hop, point, term, f1, f2, f3, stack, lead), "v" * 9,
    )
    came = along_z(corner, (1, 2))
    (defect,) = call(defect_kernel, "defect", (state,), 1, (corner, start, top), "vvv")
    next_defect = {2: along_z(defect, (3, 2)), 4: along_z(defect, (5, 4))}
    next_mine, _ = barrier((next_mine, defect))
    next_other = lax.ppermute(next_mine, "core", [(0, 1), (1, 0)])
    before, value = start, corner
    for z in (2, 4, 6):
        before, value = call(
            functools.partial(one_kernel, z), f"one{z}", (state, state), 1,
            (came, before, value, top, defect), "vvvvv", alias={1: 0, 2: 1},
        )
        if z < 6:
            (ahead,) = call(
                functools.partial(next_kernel, z), f"next{z}", (state,), 0,
                (value, next_mine, next_other, next_defect[z]), "vvvv",
                [pltpu.VMEM(WHOLE, jnp.bfloat16)],
            )
            came = along_z(ahead, (z, z + 2))
    came = along_z(value, (2, 3), (4, 5), (6, 7))
    (states,) = call(
        last_kernel, "last", (jax.ShapeDtypeStruct((4, ROWS, CH), jnp.float32),), 6,
        (came, before, value, defect, biases, stack, lead, kept), "v" * 8,
        [buffer, pltpu.VMEM((4, ROWS, CH), jnp.float32), dma((4,))], out_places="h",
    )
    volume = (8, 8, 8, CH)
    return states.reshape((4, 1) + volume), residual.reshape((1, 1) + volume)


def solution(mesh):
    finer = Mesh(mesh.devices.reshape(Z, X, 4, 2), LAYER + BATCH)
    return jax.shard_map(
        shards,
        mesh=finer,
        in_specs=(P(BATCH), P(LAYER, BATCH), P(LAYER), P(LAYER)),
        out_specs=(P(LAYER, BATCH), P(LAYER, BATCH)),
        check_vma=False,
    )
```

```python
import functools

import jax
import jax.numpy as jnp
from jax import lax
from jax.experimental import pallas as pl
from jax.experimental.pallas import tpu as pltpu
from jax.sharding import Mesh
from jax.sharding import PartitionSpec as P

X, Z = 4, 8
LAYER, BATCH = ("z", "x"), ("y", "core")
ROWS, CH = 512, 128
TAPS, DEEP = 9, 384
SHARE = TAPS * DEEP // 8
WHOLE = (8, SHARE, CH)
FINE = 2.0 / 128
COARSE = 4 * FINE
TOP = 4 * COARSE


def conv(v, weights):
    t = jnp.tanh(v).reshape(64, 8, CH)
    at = lax.broadcasted_iota(jnp.int32, (64, 8, CH), 1)
    before = jnp.where(at == 0, 0.0, pltpu.roll(t, 1, 1))
    after = jnp.where(at == 7, 0.0, pltpu.roll(t, 7, 1))
    lhs = jnp.concatenate(
        [s.reshape(ROWS, CH).astype(jnp.bfloat16) for s in (before, t, after)], 1
    )
    taps = [weights[n * DEEP : (n + 1) * DEEP] for n in range(TAPS)]
    first, second = (
        jnp.dot(lhs, jnp.concatenate(part, 1), preferred_element_type=jnp.float32)
        for part in (taps[:6], taps[6:])
    )
    edge_y = jnp.zeros((8, 1, 8, CH), jnp.float32)
    edge_x = jnp.zeros((1, 8, 8, CH), jnp.float32)
    total = None
    for dx in range(3):
        for dy in range(3):
            n = dx * 3 + dy
            part = (first if n < 6 else second)[:, n % 6 * CH : (n % 6 + 1) * CH].reshape(8, 8, 8, CH)
            if dy == 0:
                part = jnp.concatenate([edge_y, part[:, :7]], 1)
            if dy == 2:
                part = jnp.concatenate([part[:, 1:], edge_y], 1)
            if dx == 0:
                part = jnp.concatenate([edge_x, part[:7]], 0)
            if dx == 2:
                part = jnp.concatenate([part[1:], edge_x], 0)
            total = part if total is None else total + part
    return total.reshape(ROWS, CH)


def flat(weights):
    return weights.reshape(TAPS * DEEP, CH)


def last_device():
    return (lax.axis_index("x") == X - 1) & (lax.axis_index("z") == Z - 1)


def first_device():
    return (lax.axis_index("x") == 0) & (lax.axis_index("z") == 0)


def prepare_kernel(guess, inputs, kernels, corner, share, sem):
    two = pltpu.make_async_copy(
        kernels.at[0, lax.axis_index("y") * 2 + lax.axis_index("core")], share, sem.at[1]
    )
    two.start()

    @pl.when(last_device())
    def _():
        pltpu.make_async_copy(inputs, corner, sem.at[0]).start()

    @pl.when(jnp.logical_not(last_device()))
    def _():
        pltpu.make_async_copy(guess.at[3], corner, sem.at[0]).start()

    pltpu.make_async_copy(inputs, corner, sem.at[0]).wait()
    two.wait()


def load_kernel(kernels, kept, sem):
    copy = pltpu.make_async_copy(kernels, kept, sem)
    copy.start()
    copy.wait()


def first_kernel(head, kernels, biases, out):
    out[...] = head[...]

    def body(i, carry):
        v = out[...]
        out[...] = v + FINE * (conv(v, flat(kernels[pl.ds(i, 1)])) + biases[pl.ds(i, 1)])
        return carry

    lax.fori_loop(0, 4, body, 0)


def second_kernel(head, guess_head, kernels, biases, message, term, buf):
    @pl.when(first_device())
    def _():
        buf[...] = guess_head[...]

    @pl.when(jnp.logical_not(first_device()))
    def _():
        buf[...] = head[...]

    term[...] = buf[...]

    def body(i, carry):
        v = buf[...]
        mixed = conv(v, flat(kernels[pl.ds(i, 1)]))
        buf[...] = v + FINE * (mixed + biases[pl.ds(i, 1)])

        @pl.when(i == 0)
        def _():
            term[...] += COARSE * mixed

        return carry

    lax.fori_loop(0, 4, body, 0)
    term[...] = buf[...] - term[...]
    x = lax.axis_index("x")

    @pl.when(x == 0)
    def _():
        message[...] = buf[...]

    @pl.when(x > 0)
    def _():
        message[...] = term[...]


def coarse_steps(out, stack, lead, first=0, ready=lambda q: None):
    def body(q, carry):
        ready(q)
        v = out[...]
        mixed = conv(v, flat(lead[pl.ds(q, 1)]))
        out[...] = v + COARSE * mixed + stack[pl.ds(q, 1)].reshape(ROWS, CH)
        return carry

    lax.fori_loop(first, X, body, 0)


def third_kernel(
    m0, m1, m2, m3, kernels, p0, p1, p2, p3, o0, o1, o2, o3, out, stack, lead, top, part
):
    x, y, core = lax.axis_index("x"), lax.axis_index("y"), lax.axis_index("core")
    lead[pl.ds(x, 1)] = kernels[pl.ds(0, 1)]
    for offset, mine, other in ((0, p0, o0), (3, p1, o1), (1, p2, o2), (2, p3, o3)):
        at = lax.rem(y + offset, 4) * 2
        for r in range(1, X):
            q = pl.ds(lax.rem(x + r, X), 1)
            lead[q, pl.ds(at + core, 1)] = mine[r - 1].reshape(1, 1, SHARE, CH)
            lead[q, pl.ds(at + 1 - core, 1)] = other[r - 1].reshape(1, 1, SHARE, CH)
    for r, term in enumerate((m0, m1, m2, m3)):
        stack[pl.ds(lax.rem(x + r, X), 1)] = term[...].reshape(1, ROWS, CH)
    out[...] = stack[0]
    coarse_steps(out, stack, lead, 1)
    top[...] = lead[X - 1]
    part[...] = lead[X - 1, pl.ds(core * 4, 4)]


def fourth_kernel(
    inputs, hop, point, term, f1, f2, f3, stack, lead, residual, corner, start, out_stack
):
    x, z = lax.axis_index("x"), lax.axis_index("z")
    out_stack[1:] = stack[1:]
    for r, first in enumerate((term, f1, f2, f3)):

        @pl.when(x == r)
        def _():
            out_stack[0] = first[...]


    @pl.when(z == 0)
    def _():
        start[...] = inputs[...]

    @pl.when(z > 0)
    def _():
        start[...] = hop[...]

    corner[...] = start[...]
    coarse_steps(corner, out_stack, lead)

    @pl.when(x == X - 1)
    def _():
        residual[...] = corner[...] - point[...]

    @pl.when(x != X - 1)
    def _():
        residual[...] = jnp.zeros((ROWS, CH), jnp.float32)


def defect_kernel(corner, start, top, defect):
    v = start[...]
    defect[...] = corner[...] - v - TOP * conv(v, flat(top[...]))


def one_kernel(z, came, before, value, top, defect, out_before, out_value):
    @pl.when(lax.axis_index("z") == z)
    def _():
        v = came[...]
        out_before[...] = v
        out_value[...] = v + TOP * conv(v, flat(top[...])) + defect[...]


def next_kernel(z, value, mine, other, defect, ahead, wbuf):
    @pl.when(lax.axis_index("z") == z)
    def _():
        core = lax.axis_index("core")
        wbuf[pl.ds(core * 4, 4)] = mine[...]
        wbuf[pl.ds(4 - core * 4, 4)] = other[...]
        v = value[...]
        ahead[...] = v + TOP * conv(v, flat(wbuf[...])) + defect[...]


def last_kernel(came, before, value, defect, biases, stack, lead, kernels, states, buf, sbuf, sem):
    x, z = lax.axis_index("x"), lax.axis_index("z")
    late = (z == 3) | (z == 5) | (z == 7)
    extra = (x == X - 1) & late

    @pl.when(late)
    def _():
        buf[...] = came[...]

    @pl.when(jnp.logical_not(late))
    def _():
        buf[...] = before[...]

    @pl.when((x == X - 1) & jnp.logical_not(late))
    def _():
        sbuf[3] = value[...]

    @pl.when(extra)
    def _():
        v = buf[...]
        sbuf[3] = v + TOP * conv(v, flat(lead[3])) + defect[...]

    def coarse(q, carry):
        v = buf[...]
        mixed = conv(v, flat(lead[pl.ds(q, 1)]))
        buf[...] = v + COARSE * mixed + stack[pl.ds(q, 1)].reshape(ROWS, CH)
        return carry

    lax.fori_loop(0, x, coarse, 0)

    def fine(i, carry):
        v = buf[...]
        mixed = conv(v, flat(kernels[pl.ds(i, 1)]))

        @pl.when((i == 0) & (x < X - 1))
        def _():
            sbuf[3] = v + COARSE * mixed + stack[pl.ds(x, 1)].reshape(ROWS, CH)

        @pl.when(i == 0)
        def _():
            pltpu.make_async_copy(sbuf.at[3], states.at[3], sem.at[3]).start()

        new = v + FINE * (mixed + biases[pl.ds(i, 1)])
        buf[...] = new
        sbuf[pl.ds(i, 1)] = new.reshape(1, ROWS, CH)
        pltpu.make_async_copy(sbuf.at[i], states.at[i], sem.at[i]).start()
        return carry

    lax.fori_loop(0, 3, fine, 0)
    for i in range(4):
        pltpu.make_async_copy(sbuf.at[i], states.at[i], sem.at[i]).wait()


def call(body, name, outs, convs, args, places, scratch=(), alias=None, out_places=None, limit=16):
    specs = {
        "v": pl.BlockSpec(memory_space=pltpu.VMEM),
        "h": pl.BlockSpec(memory_space=pltpu.HBM),
    }
    out_places = out_places or "v" * len(outs)
    return pl.pallas_call(
        body,
        name=name,
        out_shape=outs,
        in_specs=[specs[p] for p in places],
        out_specs=tuple(specs[p] for p in out_places),
        scratch_shapes=scratch,
        input_output_aliases=alias or {},
        compiler_params=pltpu.CompilerParams(vmem_limit_bytes=limit << 20),
        cost_estimate=pl.CostEstimate(
            flops=convs if convs != 1 else 6 * 10**9,
            bytes_accessed=convs if convs != 1 else 20 * 10**6,
            transcendentals=0,
        ),
    )(*args)


def shards(inputs, guess_states, kernels, biases):
    state = jax.ShapeDtypeStruct((ROWS, CH), jnp.float32)
    weight = jax.ShapeDtypeStruct(WHOLE, jnp.bfloat16)
    buffer = pltpu.VMEM((ROWS, CH), jnp.float32)
    dma = pltpu.SemaphoreType.DMA
    inputs = inputs.reshape(ROWS, CH)
    guess = guess_states.reshape(4, ROWS, CH)
    kernels = kernels.reshape((4,) + WHOLE)
    barrier = lax.optimization_barrier

    def next_layer(v):
        return lax.ppermute(v, LAYER, [(i, (i + 1) % (X * Z)) for i in range(X * Z)])

    def from_ahead(v, r):
        return lax.ppermute(v, "x", [(i, (i - r) % X) for i in range(X)])

    def along_z(v, *pairs):
        return lax.ppermute(v, "z", pairs)

    guess_corner, share = call(
        prepare_kernel, "prepare",
        (state, jax.ShapeDtypeStruct((SHARE, CH), jnp.bfloat16)), 0,
        (guess, inputs, kernels), "hhh", [dma((2,))], limit=63,
    )
    guess_head = next_layer(guess_corner)
    shares = [from_ahead(share, 1), None, from_ahead(share, 3)]
    (kept,) = call(
        load_kernel, "load", (jax.ShapeDtypeStruct((4,) + WHOLE, jnp.bfloat16),), 0,
        (barrier((kernels, guess_corner))[0],), "h", [dma(())],
    )
    shares[1] = from_ahead(barrier((shares[0], kept))[0], 1)
    (point,) = call(
        first_kernel, "first", (state,), 4, (guess_head, kept, biases), "vvv",
    )
    head = next_layer(point)
    first_piece = jnp.stack(barrier((point, *shares))[1:])
    pieces = [first_piece] + [
        lax.ppermute(first_piece, "y", [(i, (i + r) % 4) for i in range(4)]) for r in (1, 3, 2)
    ]
    message, term = call(
        second_kernel, "second", (state, state), 4,
        (head, guess_head, kept, biases),
        "vvvv", [buffer],
    )
    m2, m3, m1 = (from_ahead(message, r) for r in (2, 3, 1))
    pieces, m2, m3 = barrier((pieces, m2, m3))
    pieces += [lax.ppermute(p, "core", [(0, 1), (1, 0)]) for p in pieces]
    term, m3 = barrier((term, m3))
    f1, f3 = (lax.ppermute(term, "x", [(0, r)]) for r in (1, 3))
    stacked = jax.ShapeDtypeStruct((X, ROWS, CH), jnp.float32)
    point, stack, lead, top, part = call(
        third_kernel, "third",
        (state, stacked, jax.ShapeDtypeStruct((X,) + WHOLE, jnp.bfloat16), weight,
         jax.ShapeDtypeStruct((4, SHARE, CH), jnp.bfloat16)),
        3, (message, m1, m2, m3, kept, *pieces), "v" * 13,
    )
    hop = along_z(point, *((i, i + 1) for i in range(Z - 1)))
    f1, hop_point = barrier((f1, point))
    f2 = lax.ppermute(f1, "x", [(1, 2)])
    next_mine = along_z(part, (3, 2), (5, 4))
    residual, corner, start, stack = call(
        fourth_kernel, "fourth", (state,) * 3 + (stacked,), 1,
        (inputs, hop, point, term, f1, f2, f3, stack, lead), "v" * 9,
    )
    came = along_z(corner, (1, 2))
    (defect,) = call(defect_kernel, "defect", (state,), 1, (corner, start, top), "vvv")
    next_defect = {2: along_z(defect, (3, 2)), 4: along_z(defect, (5, 4))}
    next_mine, _ = barrier((next_mine, defect))
    next_other = lax.ppermute(next_mine, "core", [(0, 1), (1, 0)])
    before, value = start, corner
    for z in (2, 4, 6):
        before, value = call(
            functools.partial(one_kernel, z), f"one{z}", (state, state), 1,
            (came, before, value, top, defect), "vvvvv", alias={1: 0, 2: 1},
        )
        if z < 6:
            (ahead,) = call(
                functools.partial(next_kernel, z), f"next{z}", (state,), 0,
                (value, next_mine, next_other, next_defect[z]), "vvvv",
                [pltpu.VMEM(WHOLE, jnp.bfloat16)],
            )
            came = along_z(ahead, (z, z + 2))
    came = along_z(value, (2, 3), (4, 5), (6, 7))
    (states,) = call(
        last_kernel, "last", (jax.ShapeDtypeStruct((4, ROWS, CH), jnp.float32),), 6,
        (came, before, value, defect, biases, stack, lead, kept), "v" * 8,
        [buffer, pltpu.VMEM((4, ROWS, CH), jnp.float32), dma((4,))], out_places="h",
    )
    volume = (8, 8, 8, CH)
    return states.reshape((4, 1) + volume), residual.reshape((1, 1) + volume)


def solution(mesh):
    finer = Mesh(mesh.devices.reshape(Z, X, 4, 2), LAYER + BATCH)
    return jax.shard_map(
        shards,
        mesh=finer,
        in_specs=(P(BATCH), P(LAYER, BATCH), P(LAYER), P(LAYER)),
        out_specs=(P(LAYER, BATCH), P(LAYER, BATCH)),
        check_vma=False,
    )
```
